256 devices in a mesh: layer: 32 (over x, z), plane: 8 (over y, core).
Axes of the slice: x: 4, y: 4, z: 8, core: 2. Of those that a mesh axis runs over, the one named last changes fastest.
Arguments:
- sources: float32 [32, 16, 8192], P('layer', None, 'plane'), may hold values from -6 to 6
- fronts: float32 [32, 64, 128, 128], P('layer', 'plane'), as said below
- down_left: bfloat16 [32, 8, 128, 8192], P('layer', None, None, 'plane'), may hold values from -0.1875 to 0.1875
- down_right: bfloat16 [32, 8, 128, 8192], P('layer', None, None, 'plane'), may hold values from -0.25 to 0.25
- up_left: bfloat16 [32, 8, 128, 8192], P('layer', None, None, 'plane'), may hold values from -0.1875 to 0.1875
- up_right: bfloat16 [32, 8, 128, 8192], P('layer', None, None, 'plane'), may hold values from -0.25 to 0.25
- ranks: int32 [32, 2, 8, 8], P('layer', None, 'plane'), may hold values from 1 to 128
- pattern: int32 [32, 2, 8, 8], P('layer', None, 'plane'), may hold values 0 or 1
Outputs:
- field: float32 [32, 16, 8192], P('layer', None, 'plane')
The draws below stay inside these ranges and needn't reach their ends.
Inputs may be any that keep to these rules, and one draw needn't show every extreme that they name: fronts[l, b] is lower triangular with every diagonal entry between 1 and 4.
All inputs are finite; a program needn't handle non-finite values. No bound on the sum of `pattern` on one device may be relied on, other than what follows from the above.
Results may differ from the reference program's by a relative error of at most 0.025.
Values may be sent and summed in bfloat16 or wider, within the bound.
A program may use at most 64 MiB of HBM per device.

```python
import math
import jax
import jax.numpy as jnp
from jax import lax

TILE = 1024
SOURCES = 16
RMAX = 128
BLK = 128
NT = 8
W = 8192
LAYERS = 32


def draw_fronts(key, part):
    first_key, second_key = jax.random.split(jax.random.fold_in(key, 17))
    shape = (LAYERS, W // BLK, BLK, BLK)
    lower = jax.random.normal(first_key, shape, jnp.float32) * (0.3 / math.sqrt(BLK))
    diagonal = jax.random.uniform(second_key, shape[:3], jnp.float32, 1.0, 2.0)
    identity = jnp.eye(BLK, dtype=jnp.float32)
    return jnp.tril(lower, -1) + diagonal[..., None] * identity


def set_ends(values, own_key, least, top_value):
    shape = values.shape
    index_at = [jax.random.randint(jax.random.fold_in(own_key, axis), (), 0, shape[axis]) for axis in range(len(shape))]
    values = values.at[tuple(index_at)].set(least)
    longest = shape.index(max(shape))
    index_at[longest] = (index_at[longest] + 1) % shape[longest]
    return values.at[tuple(index_at)].set(top_value)


def block_levels(own_key, shape, shards, least, top_value):
    level = 1.0
    for position, shards_of in shards:
        heights = jax.random.uniform(jax.random.fold_in(jax.random.fold_in(own_key, 6), position), (shards_of,), jnp.float32, least / len(shards), top_value / len(shards))
        level = level * jnp.repeat(jnp.exp(heights), shape[position] // shards_of).reshape((-1,) + (1,) * (len(shape) - 1 - position))
    return level


def bell_draw(rng, extent, deviation, reach, pieces=(), kind=jnp.bfloat16):
    level = block_levels(rng, extent, pieces, -0.22, 0.18) if pieces else 1.0
    drawn = jax.random.normal(rng, extent, jnp.float32) * deviation * level
    return jnp.minimum(jnp.maximum(drawn, -reach), reach).astype(kind)


def setup_inputs(seed: int = 0) -> dict:
    keys = jax.random.split(jax.random.key(seed), 9)
    return {
        "sources": bell_draw(keys[0], (LAYERS, SOURCES, W), 1.0, 6.0, ((0, 32), (2, 8)), jnp.float32),
        "fronts": draw_fronts(jax.random.fold_in(keys[8], 71), 0),
        "down_left": bell_draw(keys[2], (LAYERS, NT, RMAX, W), TILE ** -0.5, 0.1875, ((0, 32), (3, 8))),
        "down_right": bell_draw(keys[3], (LAYERS, NT, RMAX, W), (NT * RMAX * 3 // 7) ** -0.5, 0.25, ((0, 32), (3, 8))),
        "up_left": bell_draw(keys[4], (LAYERS, NT, RMAX, W), TILE ** -0.5, 0.1875, ((0, 32), (3, 8))),
        "up_right": bell_draw(keys[5], (LAYERS, NT, RMAX, W), (NT * RMAX * 3 // 7) ** -0.5, 0.25, ((0, 32), (3, 8))),
        "ranks": set_ends(jax.random.randint(keys[6], (LAYERS, 2, NT, NT), 1, RMAX + 1), jax.random.fold_in(keys[6], 1), 1, RMAX).astype(jnp.int32),
        "pattern": set_ends((jax.random.randint(keys[7], (LAYERS, 2, NT, NT), 0, 4) < 3).astype(jnp.int32), jax.random.fold_in(keys[7], 1), 0, 1),
    }


def front_solve(source, front_blocks):
    stacked = source.reshape(source.shape[0], front_blocks.shape[0], front_blocks.shape[1]).transpose(1, 2, 0)
    solved = jax.scipy.linalg.solve_triangular(front_blocks, stacked, lower=True)
    return solved.transpose(2, 0, 1).reshape(source.shape)

def transfer(trace, factor_in, factor_out, rank_rows, present):
    rounded = trace.astype(jnp.bfloat16).astype(jnp.float32).reshape(SOURCES, NT, TILE)
    left_full = factor_in.astype(jnp.float32).reshape(NT, RMAX, NT, TILE)
    coeffs = jnp.einsum('ikjt,sjt->ijsk', left_full, rounded, precision=lax.Precision.HIGHEST)
    coeffs = coeffs.astype(jnp.bfloat16).astype(jnp.float32)
    ladder = jnp.arange(RMAX, dtype=jnp.int32)
    keep_mask = present[:, :, None].astype(jnp.float32) * (ladder[None, None, :] < rank_rows[:, :, None]).astype(jnp.float32)
    coeffs = coeffs * keep_mask[:, :, None, :]
    right_full = factor_out.astype(jnp.float32).reshape(NT, RMAX, NT, TILE)
    result = jnp.einsum('ijsk,jkit->sit', coeffs, right_full, precision=lax.Precision.HIGHEST)
    return result.reshape(SOURCES, W)

def reference(sources, fronts, down_left, down_right, up_left, up_right, ranks, pattern):
    solved = jax.vmap(front_solve)(sources, fronts)

    def sweep_step(previous, items):
        local_part, factor_in, factor_out, rank_rows, present = items
        nxt = local_part + transfer(previous, factor_in, factor_out, rank_rows, present)
        return (nxt, nxt)
    start = jnp.zeros((SOURCES, W), jnp.float32)
    _, down = lax.scan(sweep_step, start, (solved, down_left, down_right, ranks[:, 0], pattern[:, 0]))
    _, upward = lax.scan(sweep_step, start, (solved, up_left, up_right, ranks[:, 1], pattern[:, 1]), reverse=True)
    return down + upward - solved
```

```python
import jax
import jax.numpy as jnp
from jax import lax
from jax.experimental import pallas as pl
from jax.experimental.pallas import tpu as pltpu
from jax.sharding import PartitionSpec as P

MESH = pl.DeviceIdType.MESH
BF16, F32 = jnp.bfloat16, jnp.float32
LAYERS, CHIPS, SOURCES = 32, 4, 16
LAST = LAYERS - 1
SEND_EARLY, MAKE_EARLY = 8, 10
NT = (((1,), (1,)), ((), ()))


def piece_row(ref):
    return jnp.concatenate([ref[j] for j in range(8)], axis=1)


def kernel(
    sources, fronts, down_left, down_right, up_left, up_right, ranks, pattern, out,
    src, tri, solved, solved_even, solved_odd, kept, even_right, odd_right, even_left, odd_left,
    even_step, odd_step, even_start, odd_start, even_in, odd_in, own_in, sent,
    load_sem, kept_sem, left_sem, solved_sem, sent_sem, relay_sem,
    even_right_got, odd_right_got, even_left_got, solved_even_got, solved_odd_got, even_in_got, odd_in_got, own_in_got, go_sem,
):
    layer, plane = lax.axis_index("layer"), lax.axis_index("plane")
    y, core = plane // 2, lax.rem(plane, 2)
    is_odd = core == 1
    odd_plane = 2 * y + 1
    upper = (layer >= LAYERS // 2).astype(jnp.int32)
    first, second = upper, 1 - upper
    lefts, rights = (down_left, up_left), (down_right, up_right)

    def sign(d):
        return 1 - 2 * d

    def position(d):
        return jnp.where(d == 0, layer, LAST - layer)

    def remote(source, target, send, got, to_layer, to_plane):
        return pltpu.make_async_remote_copy(
            source, target, send, got, device_id=(to_layer, to_plane), device_id_type=MESH
        )

    load_tri = pltpu.make_async_copy(fronts.at[0], tri, load_sem.at[0])
    load_src = pltpu.make_async_copy(sources.at[0], src, load_sem.at[1])
    load_right = [pltpu.make_async_copy(rights[d].at[0], kept.at[d], load_sem.at[2 + d]) for d in range(2)]
    load_left = [pltpu.make_async_copy(lefts[d].at[0], odd_left.at[d], load_sem.at[4 + d]) for d in range(2)]
    for copy in load_right:
        copy.start()
    load_tri.start()
    load_src.start()
    for copy in load_left:
        copy.start()

    barrier = pltpu.get_barrier_semaphore()

    def greet(to_layer, to_plane):
        pl.semaphore_signal(barrier, inc=1, device_id=(to_layer, to_plane), device_id_type=MESH)

    def reach(r):
        return jnp.minimum(layer + r, LAST) - jnp.maximum(layer - r, 0) + 1

    @pl.when(is_odd)
    def _():
        for by in (-2, -1, 1, 2):

            @pl.when((layer + by >= 0) & (layer + by <= LAST))
            def _():
                for other in range(CHIPS):
                    greet(layer + by, 2 * other + 1)

        for turn in range(1, CHIPS):
            greet(layer, 2 * lax.rem(y + turn, CHIPS) + 1)
        for by in (-1, 0, 1):

            @pl.when((layer + by >= 0) & (layer + by <= LAST))
            def _():
                greet(layer + by, 2 * y)

        pl.semaphore_wait(barrier, CHIPS * reach(2) - 1 + reach(1))

    @pl.when(core == 0)
    def _():
        for by in (-1, 0, 1):

            @pl.when((layer + by >= 0) & (layer + by <= LAST))
            def _():
                greet(layer + by, odd_plane)

        pl.semaphore_wait(barrier, reach(1))

    def send_left(d, start):
        for way in range(2):

            @pl.when((core == 0) & (d == way) & (position(way) >= 1))
            def _():
                copy = remote(
                    lefts[way].at[0], even_left.at[way], left_sem.at[way], even_left_got.at[way],
                    layer - sign(way), odd_plane,
                )
                if start:
                    copy.start()
                else:
                    copy.wait_send()

    def send_right(d, start):
        even = remote(kept.at[d], even_right.at[d], kept_sem.at[d], even_right_got.at[d], layer, odd_plane)
        odd = remote(kept.at[d], odd_right.at[d], kept_sem.at[d], odd_right_got.at[d], layer + sign(d), odd_plane)

        @pl.when(core == 0)
        def _():
            if start:
                even.start()
            else:
                even.wait_send()

        @pl.when(is_odd & (position(d) < LAST))
        def _():
            if start:
                odd.start()
            else:
                odd.wait_send()

    def mask_right(d):
        for j in range(8):
            top = ranks[0, d, 0, j] * pattern[0, d, 0, j]
            rows = lax.broadcasted_iota(jnp.int32, (128, 1024), 0)
            kept[d, j] = jnp.where(rows < top, kept[d, j].astype(F32), 0.0).astype(BF16)

    send_left(first, True)
    for copy in load_right:
        copy.wait()
    mask_right(first)
    send_right(first, True)
    mask_right(second)

    load_tri.wait()
    load_src.wait()
    row = lax.broadcasted_iota(jnp.int32, (128, 128), 0)
    col = lax.broadcasted_iota(jnp.int32, (128, 128), 1)

    def exact(a, b):
        return jnp.dot(a, b, preferred_element_type=F32, precision=lax.Precision.HIGHEST)

    for b in range(8):
        block = tri[b]
        diagonal = jnp.where(row == col, block, 0.0)
        by_row = 1.0 / jnp.sum(diagonal, axis=1, keepdims=True)
        by_col = 1.0 / jnp.sum(diagonal, axis=0, keepdims=True)
        unit = jnp.where(row > col, block * by_row, 0.0)
        inverse = jnp.where(row == col, 1.0, 0.0)
        half = 1
        while half < 128:
            joins = (row // (2 * half) == col // (2 * half)) & (row // half != col // half)
            part = jnp.where(joins, unit, 0.0)
            if half == 1:
                inverse = inverse - part
            else:
                inverse = inverse - exact(inverse, exact(part, inverse))
            half *= 2
        scaled = src[:, 128 * b : 128 * (b + 1)] * by_col
        solved[:, 128 * b : 128 * (b + 1)] = lax.dot_general(
            scaled, inverse, NT, preferred_element_type=F32, precision=lax.Precision.HIGHEST
        )
    sent_solved = solved_odd.at[2]
    sent_solved[...] = solved[...].astype(BF16)
    even_solved = remote(sent_solved, solved_even, solved_sem.at[0], solved_even_got, layer, odd_plane)

    def odd_solved(d):
        return remote(
            sent_solved, solved_odd.at[d], solved_sem.at[d], solved_odd_got.at[d], layer + sign(d), odd_plane
        )

    @pl.when(core == 0)
    def _():
        even_solved.start()

    for d in range(2):

        @pl.when(is_odd & (position(d) < LAST))
        def _():
            odd_solved(d).start()

    for copy in load_left:
        copy.wait()
    send_left(first, False)
    send_right(first, False)

    def send_second():
        send_left(second, True)
        send_right(second, True)

    @pl.when(position(first) >= SEND_EARLY)
    def _():
        send_second()

    def make(right, left, d, solution_part, step, start):
        @pl.loop(0, CHIPS)
        def _(chip):
            block = left[d, pl.ds(2 * chip, 2)].reshape(256, 1024)
            full = right[d].reshape(1024, 1024)
            step[d, chip] = lax.dot_general(full, block, NT, preferred_element_type=F32).astype(BF16)
            start[d, chip] = lax.dot_general(solution_part, block, NT, preferred_element_type=F32)

    def prepare(d):
        q = position(d)

        @pl.when(q >= 1)
        def _():
            remote(kept.at[d], odd_right.at[d], kept_sem.at[d], odd_right_got.at[d], layer, odd_plane).wait_recv()
            remote(sent_solved, solved_odd.at[d], solved_sem.at[d], solved_odd_got.at[d], layer, odd_plane).wait_recv()
            make(odd_right, odd_left, d, solved_odd[d], odd_step, odd_start)

        remote(kept.at[d], even_right.at[d], kept_sem.at[d], even_right_got.at[d], layer, odd_plane).wait_recv()

        @pl.when(q < LAST)
        def _():
            remote(even_left.at[d], even_left.at[d], left_sem.at[d], even_left_got.at[d], layer, odd_plane).wait_recv()
            make(even_right, even_left, d, solved_even[...], even_step, even_start)

    def advance(d, event, values, step, start, deliver):
        for turn in (2, 1, 3, 0):
            other = lax.rem(y + turn, CHIPS)
            result = start[d, other]
            if values is not None:
                result = result + jnp.dot(values, step[d, other], preferred_element_type=F32)
            result = result.astype(BF16)
            deliver(turn, other, result)

    def wait_pieces(ref, got, count):
        remote(ref.at[pl.ds(0, count)], ref.at[pl.ds(0, count)], sent_sem.at[0], got, layer, odd_plane).wait_recv()

    def run_odd(d):
        q = position(d)

        def deliver(turn, other, result):
            for part in range(2):
                sent[d, 1, other, part] = result[:, 128 * part : 128 * (part + 1)]
            if turn == 0:
                even_in[d, odd_plane] = result[:, :128]
            else:
                remote(
                    sent.at[d, 1, other, 0], even_in.at[d, odd_plane], sent_sem.at[d], even_in_got.at[d],
                    layer, 2 * other + 1,
                ).start()

            @pl.when(q < LAST)
            def _():
                remote(
                    sent.at[d, 1, other, 1], odd_in.at[d, odd_plane], sent_sem.at[d], odd_in_got.at[d],
                    layer + sign(d), 2 * other + 1,
                ).start()

            @pl.when(q == LAST)
            def _():
                if turn == 0:
                    own_in[d, odd_plane] = result[:, 128:]
                else:
                    remote(
                        sent.at[d, 1, other, 1], own_in.at[d, odd_plane], sent_sem.at[d], own_in_got.at[d],
                        layer, 2 * other + 1,
                    ).start()

        @pl.when(q == 1)
        def _():
            advance(d, 1, None, odd_step, odd_start, deliver)

        @pl.when(q >= 2)
        def _():
            wait_pieces(odd_in.at[d], odd_in_got.at[d], 8)
            advance(d, 1, piece_row(odd_in.at[d]), odd_step, odd_start, deliver)

    def run_even(d):
        q = position(d)

        def deliver(turn, other, result):
            for part in range(2):
                sent[d, 0, other, part] = result[:, 128 * part : 128 * (part + 1)]
            remote(
                sent.at[d, 0, other, 0], even_in.at[d, 2 * y], sent_sem.at[d], even_in_got.at[d],
                layer + sign(d), 2 * other + 1,
            ).start()

            @pl.when(q < LAST - 1)
            def _():
                remote(
                    sent.at[d, 0, other, 1], odd_in.at[d, 2 * y], sent_sem.at[d], odd_in_got.at[d],
                    layer + 2 * sign(d), 2 * other + 1,
                ).start()

            @pl.when(q == LAST - 1)
            def _():
                remote(
                    sent.at[d, 0, other, 1], own_in.at[d, 2 * y], sent_sem.at[d], own_in_got.at[d],
                    layer + sign(d), 2 * other + 1,
                ).start()

        @pl.when(q == 0)
        def _():
            advance(d, 0, None, even_step, even_start, deliver)

        @pl.when(q >= 1)
        def _():
            wait_pieces(even_in.at[d], even_in_got.at[d], 7)

        @pl.when((q >= 1) & (q < LAST))
        def _():
            advance(d, 0, piece_row(even_in.at[d]), even_step, even_start, deliver)

    def relay_even(d):
        return remote(even_in.at[d], own_in.at[d], relay_sem.at[0, d], own_in_got.at[d], layer, 2 * y)

    def relay_odd(d):
        return remote(odd_in.at[d], own_in.at[d], relay_sem.at[1, d], own_in_got.at[d], layer - sign(d), odd_plane)

    def sweep(d):
        q = position(d)
        run_odd(d)
        run_even(d)

        @pl.when(q >= 1)
        def _():
            relay_even(d).start()

        @pl.when(q >= 2)
        def _():
            relay_odd(d).start()

    @pl.when(is_odd)
    def _():
        remote(sent_solved, solved_even, solved_sem.at[0], solved_even_got, layer, odd_plane).wait_recv()
        prepare(first)

        @pl.when(position(first) >= MAKE_EARLY)
        def _():
            prepare(second)

        sweep(first)

        @pl.when(position(first) < SEND_EARLY)
        def _():
            pl.semaphore_signal(go_sem, inc=1, device_id=(layer, 2 * y), device_id_type=MESH)
            send_second()

        @pl.when(position(first) < MAKE_EARLY)
        def _():
            prepare(second)

        sweep(second)

    @pl.when((core == 0) & (position(first) < SEND_EARLY))
    def _():
        pl.semaphore_wait(go_sem, 1)
        send_second()

    def add_own(d):
        q = position(d)

        @pl.when(q >= 1)
        def _():
            @pl.when(is_odd & (q == LAST))
            def _():
                wait_pieces(own_in.at[d], own_in_got.at[d], 7)

            @pl.when((core == 0) | (q < LAST))
            def _():
                wait_pieces(own_in.at[d], own_in_got.at[d], 8)

            solved[...] += jnp.dot(
                piece_row(own_in.at[d]), kept[d].reshape(1024, 1024), preferred_element_type=F32
            )

    add_own(first)
    add_own(second)
    out[0] = solved[...]

    send_left(second, False)
    send_right(second, False)

    @pl.when(core == 0)
    def _():
        even_solved.wait_send()

    @pl.when(is_odd)
    def _():
        for d in range(2):
            q = position(d)

            def drain(count):
                part = odd_in.at[d, pl.ds(0, count)]
                remote(part, part, sent_sem.at[d], odd_in_got.at[d], layer, odd_plane).wait_send()

            @pl.when(q < LAST)
            def _():
                odd_solved(d).wait_send()
                drain(8)

            @pl.when((q >= 1) & (q < LAST))
            def _():
                drain(7)

            @pl.when(q == LAST)
            def _():
                drain(6)

            @pl.when(q >= 1)
            def _():
                relay_even(d).wait_send()

            @pl.when(q >= 2)
            def _():
                relay_odd(d).wait_send()


def shards(*arrays):
    anywhere = pl.BlockSpec(memory_space=pl.ANY)
    scalars = pl.BlockSpec(memory_space=pltpu.SMEM)
    dma, vmem = pltpu.SemaphoreType.DMA, pltpu.VMEM
    return pl.pallas_call(
        kernel,
        name="sweep",
        out_shape=jax.ShapeDtypeStruct((1, SOURCES, 1024), F32),
        in_specs=[anywhere] * 6 + [scalars] * 2,
        out_specs=pl.BlockSpec(memory_space=pltpu.VMEM),
        scratch_shapes=[
            vmem((SOURCES, 1024), F32),
            vmem((8, 128, 128), F32),
            vmem((SOURCES, 1024), F32),
            vmem((SOURCES, 1024), BF16),
            vmem((3, SOURCES, 1024), BF16),
            vmem((2, 8, 128, 1024), BF16),
            vmem((2, 8, 128, 1024), BF16),
            vmem((2, 8, 128, 1024), BF16),
            vmem((2, 8, 128, 1024), BF16),
            vmem((2, 8, 128, 1024), BF16),
            vmem((2, CHIPS, 1024, 256), BF16),
            vmem((2, CHIPS, 1024, 256), BF16),
            vmem((2, CHIPS, SOURCES, 256), F32),
            vmem((2, CHIPS, SOURCES, 256), F32),
            vmem((2, 8, SOURCES, 128), BF16),
            vmem((2, 8, SOURCES, 128), BF16),
            vmem((2, 8, SOURCES, 128), BF16),
            vmem((2, 2, CHIPS, 2, SOURCES, 128), BF16),
            dma((6,)),
            dma((2,)),
            dma((2,)),
            dma((2,)),
            dma((2,)),
            dma((2, 2)),
            dma((2,)),
            dma((2,)),
            dma((2,)),
            dma(()),
            dma((2,)),
            dma((2,)),
            dma((2,)),
            dma((2,)),
            pltpu.SemaphoreType.REGULAR,
        ],
        compiler_params=pltpu.CompilerParams(
            collective_id=0, has_side_effects=True, vmem_limit_bytes=56 << 20
        ),
    )(*arrays)


def solution(mesh):
    in_specs = (
        P("layer", None, "plane"),
        P("layer", "plane", None, None),
        P("layer", None, None, "plane"),
        P("layer", None, None, "plane"),
        P("layer", None, None, "plane"),
        P("layer", None, None, "plane"),
        P("layer", None, "plane", None),
        P("layer", None, "plane", None),
    )
    return jax.shard_map(
        shards, mesh=mesh, in_specs=in_specs, out_specs=P("layer", None, "plane"), check_vma=False
    )
```

```python
import jax
import jax.numpy as jnp
from jax import lax
from jax.experimental import pallas as pl
from jax.experimental.pallas import tpu as pltpu
from jax.sharding import PartitionSpec as P

MESH = pl.DeviceIdType.MESH
BF16, F32 = jnp.bfloat16, jnp.float32
LAYERS, CHIPS, SOURCES = 32, 4, 16
LAST = LAYERS - 1
SEND_EARLY, MAKE_EARLY = 11, 14
SLOW = 3
NT = (((1,), (1,)), ((), ()))


def piece_row(ref):
    return jnp.concatenate([ref[j] for j in range(8)], axis=1)


def kernel(
    sources, fronts, down_left, down_right, up_left, up_right, ranks, pattern, out,
    src, tri, solved, solved_even, solved_odd, kept, even_right, odd_right, even_left, odd_left,
    even_step, odd_step, even_start, odd_start, even_in, odd_in, own_in, sent,
    slow_sent, load_sem, kept_sem, left_sem, solved_sem, sent_sem, relay_sem, slow_sem,
    even_right_got, odd_right_got, even_left_got, solved_even_got, solved_odd_got, even_in_got, odd_in_got, own_in_got, go_sem,
):
    layer, plane = lax.axis_index("layer"), lax.axis_index("plane")
    y, core = plane // 2, lax.rem(plane, 2)
    is_odd = core == 1
    odd_plane = 2 * y + 1
    upper = (layer >= LAYERS // 2).astype(jnp.int32)
    first, second = upper, 1 - upper
    lefts, rights = (down_left, up_left), (down_right, up_right)

    def sign(d):
        return 1 - 2 * d

    def position(d):
        return jnp.where(d == 0, layer, LAST - layer)

    def remote(source, target, send, got, to_layer, to_plane):
        return pltpu.make_async_remote_copy(
            source, target, send, got, device_id=(to_layer, to_plane), device_id_type=MESH
        )

    load_tri = pltpu.make_async_copy(fronts.at[0], tri, load_sem.at[0])
    load_src = pltpu.make_async_copy(sources.at[0], src, load_sem.at[1])
    def each(d, action):
        for way in range(2):
            pl.when(d == way)(lambda: action(way))

    def load_right(way):
        return pltpu.make_async_copy(rights[way].at[0], kept.at[way], load_sem.at[2 + way])

    def load_left(way):
        return pltpu.make_async_copy(lefts[way].at[0], odd_left.at[way], load_sem.at[4 + way])

    each(first, lambda way: load_right(way).start())
    load_tri.start()
    load_src.start()

    early = position(first)
    forward = sign(first)
    is_slow = (early >= 1) & (early <= SLOW)

    @pl.when(is_odd | is_slow)
    def _():
        each(first, lambda way: load_left(way).start())

    barrier = pltpu.get_barrier_semaphore()

    def greet(to_layer, to_plane):
        pl.semaphore_signal(barrier, inc=1, device_id=(to_layer, to_plane), device_id_type=MESH)

    def reach(r):
        return jnp.minimum(layer + r, LAST) - jnp.maximum(layer - r, 0) + 1

    @pl.when(is_odd)
    def _():
        for by in (-2, -1, 1, 2):

            @pl.when((layer + by >= 0) & (layer + by <= LAST))
            def _():
                for other in range(CHIPS):
                    greet(layer + by, 2 * other + 1)

        for turn in range(1, CHIPS):
            greet(layer, 2 * lax.rem(y + turn, CHIPS) + 1)
        for by in (-1, 0, 1):

            @pl.when((layer + by >= 0) & (layer + by <= LAST))
            def _():
                greet(layer + by, 2 * y)

        beside_slow = is_slow.astype(jnp.int32)
        past_slow = ((early >= 2) & (early <= SLOW + 1)).astype(jnp.int32)
        for turn in range(1, CHIPS):

            @pl.when(is_slow)
            def _():
                greet(layer, 2 * lax.rem(y + turn, CHIPS))

            @pl.when((early >= 2) & (early <= SLOW + 1))
            def _():
                greet(layer - forward, 2 * lax.rem(y + turn, CHIPS))

        pl.semaphore_wait(barrier, CHIPS * reach(2) - 1 + reach(1) + (CHIPS - 1) * (beside_slow + past_slow))

    @pl.when(core == 0)
    def _():
        for by in (-1, 0, 1):

            @pl.when((layer + by >= 0) & (layer + by <= LAST))
            def _():
                greet(layer + by, odd_plane)

        @pl.when(is_slow)
        def _():
            for turn in range(1, CHIPS):
                greet(layer, 2 * lax.rem(y + turn, CHIPS) + 1)
                greet(layer + forward, 2 * lax.rem(y + turn, CHIPS) + 1)

        @pl.when(early == 0)
        def _():
            greet(layer + forward, plane)

        @pl.when(early == 1)
        def _():
            greet(layer - forward, plane)

        pl.semaphore_wait(
            barrier, reach(1) + 2 * (CHIPS - 1) * is_slow.astype(jnp.int32) + (early <= 1).astype(jnp.int32)
        )

    def send_left(d):
        for way in range(2):

            @pl.when((core == 0) & (d == way) & (position(way) > SLOW))
            def _():
                for chip in range(CHIPS):
                    pair = pl.ds(2 * chip, 2)
                    remote(
                        lefts[way].at[0, pair], even_left.at[way, pair], left_sem.at[way], even_left_got.at[way, chip],
                        layer - sign(way), odd_plane,
                    ).start()

    def send_right(d):
        @pl.when(core == 0)
        def _():
            remote(kept.at[d], even_right.at[d], kept_sem.at[d], even_right_got.at[d], layer, odd_plane).start()

        @pl.when(is_odd & (position(d) >= SLOW) & (position(d) < LAST))
        def _():
            remote(
                kept.at[d], odd_right.at[d], kept_sem.at[d], odd_right_got.at[d], layer + sign(d), odd_plane
            ).start()

    def sent_factors(d):
        @pl.when((core == 0) & (position(d) > SLOW))
        def _():
            remote(even_left.at[d], even_left.at[d], left_sem.at[d], even_left_got.at[d, 0], layer, odd_plane).wait_send()

        @pl.when((core == 0) | ((position(d) >= SLOW) & (position(d) < LAST)))
        def _():
            remote(kept.at[d], even_right.at[d], kept_sem.at[d], even_right_got.at[d], layer, odd_plane).wait_send()

    def mask_right(d):
        for j in range(8):
            top = ranks[0, d, 0, j] * pattern[0, d, 0, j]
            rows = lax.broadcasted_iota(jnp.int32, (128, 1024), 0)
            kept[d, j] = jnp.where(rows < top, kept[d, j].astype(F32), 0.0).astype(BF16)

    send_left(first)
    each(first, lambda way: load_right(way).wait())
    mask_right(first)
    send_right(first)
    each(second, lambda way: load_right(way).start())

    @pl.when(is_odd)
    def _():
        each(second, lambda way: load_left(way).start())

    load_tri.wait()
    load_src.wait()
    row = lax.broadcasted_iota(jnp.int32, (128, 128), 0)
    col = lax.broadcasted_iota(jnp.int32, (128, 128), 1)

    def exact(a, b):
        return jnp.dot(a, b, preferred_element_type=F32, precision=lax.Precision.HIGHEST)

    by_col, units, inverses = [], [], []
    for b in range(8):
        block = tri[b]
        diagonal = jnp.where(row == col, block, 0.0)
        by_row = 1.0 / jnp.sum(diagonal, axis=1, keepdims=True)
        by_col.append(1.0 / jnp.sum(diagonal, axis=0, keepdims=True))
        units.append(jnp.where(row > col, block * by_row, 0.0))
        inverses.append(jnp.where(row == col, 1.0, 0.0))
    for half in (1, 2, 4, 8, 16, 32, 64):
        joins = (row // (2 * half) == col // (2 * half)) & (row // half != col // half)
        for b in range(8):
            part = jnp.where(joins, units[b], 0.0)
            if half > 1:
                part = exact(inverses[b], exact(part, inverses[b]))
            inverses[b] = inverses[b] - part
    for b in range(8):
        solved[:, 128 * b : 128 * (b + 1)] = lax.dot_general(
            src[:, 128 * b : 128 * (b + 1)] * by_col[b], inverses[b], NT,
            preferred_element_type=F32, precision=lax.Precision.HIGHEST,
        )
    sent_solved = solved_odd.at[2]
    sent_solved[...] = solved[...].astype(BF16)
    even_solved = remote(sent_solved, solved_even, solved_sem.at[0], solved_even_got, layer, odd_plane)

    def odd_solved(d):
        return remote(
            sent_solved, solved_odd.at[d], solved_sem.at[d], solved_odd_got.at[d], layer + sign(d), odd_plane
        )

    def sends_solved(d):
        return is_odd & (position(d) < LAST) & ((position(d) == 0) | (position(d) >= SLOW))

    def slow_even(source):
        return remote(source, solved_even, slow_sem.at[0], solved_even_got, layer + forward, 2 * y)

    def slow_odd(source):
        return remote(
            source, solved_odd.at[first], slow_sem.at[1], solved_odd_got.at[first], layer + forward, odd_plane
        )

    @pl.when((core == 0) & (early == 0))
    def _():
        slow_even(sent_solved).start()

    @pl.when(core == 0)
    def _():
        even_solved.start()

    for d in range(2):

        @pl.when(sends_solved(d))
        def _():
            odd_solved(d).start()

    each(second, lambda way: load_right(way).wait())
    mask_right(second)

    def send_second():
        sent_factors(first)
        send_left(second)
        send_right(second)

    def open_way(d):
        each(d, lambda way: load_left(way).wait())

        @pl.when(position(d) >= 1)
        def _():
            remote(sent_solved, solved_odd.at[d], solved_sem.at[d], solved_odd_got.at[d], layer, odd_plane).wait_recv()
            begin = lax.dot_general(
                solved_odd[d], odd_left[d].reshape(1024, 1024), NT, preferred_element_type=F32
            )
            for chip in range(CHIPS):
                odd_start[d, chip] = begin[:, 256 * chip : 256 * (chip + 1)]

    def wait_even_right(d):
        remote(kept.at[d], even_right.at[d], kept_sem.at[d], even_right_got.at[d], layer, odd_plane).wait_recv()

    def make(right, left, d, chip, step):
        block = left[d, pl.ds(2 * chip, 2)].reshape(256, 1024)
        full = right[d].reshape(1024, 1024)
        columns = lax.dot_general(full, block, NT, preferred_element_type=F32).astype(BF16)
        step[d, chip] = columns.reshape(CHIPS, 256, 256)

    def make_odd(d):
        @pl.when(position(d) > SLOW)
        def _():
            remote(kept.at[d], odd_right.at[d], kept_sem.at[d], odd_right_got.at[d], layer, odd_plane).wait_recv()

            @pl.loop(0, CHIPS)
            def _(chip):
                make(odd_right, odd_left, d, chip, odd_step)

    def make_even(d):
        @pl.when((position(d) >= SLOW) & (position(d) < LAST))
        def _():
            @pl.loop(0, CHIPS)
            def _(chip):
                part = even_left.at[d, pl.ds(2 * chip, 2)]
                remote(part, part, left_sem.at[d], even_left_got.at[d, chip], layer, odd_plane).wait_recv()
                block = even_left[d, pl.ds(2 * chip, 2)].reshape(256, 1024)
                even_start[d, chip] = lax.dot_general(solved_even[...], block, NT, preferred_element_type=F32)
                make(even_right, even_left, d, chip, even_step)

    def wait_pieces(ref, got, count):
        remote(ref.at[pl.ds(0, count)], ref.at[pl.ds(0, count)], sent_sem.at[0], got, layer, odd_plane).wait_recv()

    def pair_row(ref, chip):
        return jnp.concatenate([ref[2 * chip], ref[2 * chip + 1]], axis=1)

    def start_only(d, start, deliver):
        for turn in (2, 1, 3, 0):
            other = lax.rem(y + turn, CHIPS)
            deliver(turn, other, start[d, other].astype(BF16))

    def advance(d, ref, got, near, step, start, deliver):
        turns = (2, 1, 3, 0)
        others = {turn: lax.rem(y + turn, CHIPS) for turn in turns}
        wait_pieces(ref, got.at[d, 0], near)
        totals = {turn: start[d, others[turn]] for turn in turns}
        for source in (0, 1, 3):
            values = pair_row(ref, others[source])
            for turn in turns:
                totals[turn] += jnp.dot(
                    values, step[d, others[turn], others[source]], preferred_element_type=F32
                )
        wait_pieces(ref, got.at[d, 1], 2)
        values = pair_row(ref, others[2])
        for turn in turns:
            total = totals[turn] + jnp.dot(values, step[d, others[turn], others[2]], preferred_element_type=F32)
            deliver(turn, others[turn], total.astype(BF16))

    def far(turn):
        return 1 if turn == 2 else 0

    def odd_deliver(d):
        q = position(d)
        direct = (q == LAST) | (q < SLOW)

        def deliver(turn, other, result):
            for part in range(2):
                sent[d, 1, other, part] = result[:, 128 * part : 128 * (part + 1)]
            if turn == 0:
                even_in[d, odd_plane] = result[:, :128]
            else:
                remote(
                    sent.at[d, 1, other, 0], even_in.at[d, odd_plane], sent_sem.at[d], even_in_got.at[d, far(turn)],
                    layer, 2 * other + 1,
                ).start()

            @pl.when(jnp.logical_not(direct))
            def _():
                remote(
                    sent.at[d, 1, other, 1], odd_in.at[d, odd_plane], sent_sem.at[d], odd_in_got.at[d, far(turn)],
                    layer + sign(d), 2 * other + 1,
                ).start()

            @pl.when(direct)
            def _():
                if turn == 0:
                    own_in[d, odd_plane] = result[:, 128:]
                else:
                    remote(
                        sent.at[d, 1, other, 1], own_in.at[d, odd_plane], sent_sem.at[d], own_in_got.at[d],
                        layer, 2 * other + 1,
                    ).start()

        return deliver

    def run_odd(d):
        @pl.when(position(d) > SLOW)
        def _():
            advance(d, odd_in.at[d], odd_in_got, 6, odd_step, odd_start, odd_deliver(d))

    def run_even(d):
        q = position(d)

        def deliver(turn, other, result):
            for part in range(2):
                sent[d, 0, other, part] = result[:, 128 * part : 128 * (part + 1)]
            remote(
                sent.at[d, 0, other, 0], even_in.at[d, 2 * y], sent_sem.at[d], even_in_got.at[d, far(turn)],
                layer + sign(d), 2 * other + 1,
            ).start()

            @pl.when(q < LAST - 1)
            def _():
                remote(
                    sent.at[d, 0, other, 1], odd_in.at[d, 2 * y], sent_sem.at[d], odd_in_got.at[d, far(turn)],
                    layer + 2 * sign(d), 2 * other + 1,
                ).start()

            @pl.when(q == LAST - 1)
            def _():
                remote(
                    sent.at[d, 0, other, 1], own_in.at[d, 2 * y], sent_sem.at[d], own_in_got.at[d],
                    layer + sign(d), 2 * other + 1,
                ).start()

        @pl.when((q >= SLOW) & (q < LAST))
        def _():
            advance(d, even_in.at[d], even_in_got, 5, even_step, even_start, deliver)

        @pl.when(q == LAST)
        def _():
            wait_pieces(even_in.at[d], even_in_got.at[d, 0], 5)
            wait_pieces(even_in.at[d], even_in_got.at[d, 1], 2)

    def slow_deliver(turn, other, result):
        for part in range(2):
            sent[first, 0, other, part] = result[:, 128 * part : 128 * (part + 1)]
        remote(
            sent.at[first, 0, other, 0], even_in.at[first, 2 * y], sent_sem.at[first],
            even_in_got.at[first, far(turn)], layer, 2 * other + 1,
        ).start()

        @pl.when(early < SLOW)
        def _():
            remote(
                sent.at[first, 0, other, 1], own_in.at[first, 2 * y], sent_sem.at[first], own_in_got.at[first],
                layer, 2 * other + 1,
            ).start()

        @pl.when(early == SLOW)
        def _():
            remote(
                sent.at[first, 0, other, 1], odd_in.at[first, 2 * y], sent_sem.at[first],
                odd_in_got.at[first, far(turn)], layer + forward, 2 * other + 1,
            ).start()

    @pl.when((core == 0) & is_slow)
    def _():
        each(first, lambda way: load_left(way).wait())
        remote(sent_solved, solved_even, solved_sem.at[0], solved_even_got, layer, 2 * y).wait_recv()
        for turn in (2, 1, 3, 0):
            other = lax.rem(y + turn, CHIPS)
            block = odd_left[first, pl.ds(2 * other, 2)].reshape(256, 1024)
            result = lax.dot_general(solved_even[...], block, NT, preferred_element_type=F32)
            slow_deliver(turn, other, result.astype(BF16))

    def slow_step():
        wait_pieces(even_in.at[first], even_in_got.at[first, 0], 5)
        wait_pieces(even_in.at[first], even_in_got.at[first, 1], 2)
        trace = jnp.dot(
            piece_row(even_in.at[first]), even_right[first].reshape(1024, 1024), preferred_element_type=F32
        )
        slow_sent[0] = (solved_even[...].astype(F32) + trace).astype(BF16)
        slow_even(slow_sent.at[0]).start()
        wait_pieces(own_in.at[first], own_in_got.at[first], 7)
        trace = jnp.dot(
            piece_row(own_in.at[first]), kept[first].reshape(1024, 1024), preferred_element_type=F32
        )
        slow_sent[1] = (solved[...] + trace).astype(BF16)
        slow_odd(slow_sent.at[1]).start()

    def relay_even(d):
        return remote(even_in.at[d], own_in.at[d], relay_sem.at[0, d], own_in_got.at[d], layer, 2 * y)

    def relay_odd(d):
        return remote(odd_in.at[d], own_in.at[d], relay_sem.at[1, d], own_in_got.at[d], layer - sign(d), odd_plane)

    def sweep(d):
        q = position(d)
        run_even(d)

        @pl.when(q >= 1)
        def _():
            relay_even(d).start()

        @pl.when(q > SLOW)
        def _():
            relay_odd(d).start()

    @pl.when(is_odd)
    def _():
        remote(sent_solved, solved_even, solved_sem.at[0], solved_even_got, layer, odd_plane).wait_recv()
        wait_even_right(first)
        open_way(first)

        @pl.when(is_slow)
        def _():
            start_only(first, odd_start, odd_deliver(first))

        @pl.when((early >= 1) & (early < SLOW))
        def _():
            slow_step()

        @pl.when(position(first) >= SEND_EARLY)
        def _():
            send_second()

        make_odd(first)

        @pl.when(early <= SLOW + 1)
        def _():
            run_odd(first)

        make_even(first)

        @pl.when(position(first) >= MAKE_EARLY)
        def _():
            wait_even_right(second)
            open_way(second)
            make_odd(second)
            make_even(second)

        @pl.when(early > SLOW + 1)
        def _():
            run_odd(first)

        sweep(first)

        @pl.when(position(first) < SEND_EARLY)
        def _():
            pl.semaphore_signal(go_sem, inc=1, device_id=(layer, 2 * y), device_id_type=MESH)
            send_second()

        @pl.when(position(first) < MAKE_EARLY)
        def _():
            wait_even_right(second)
            open_way(second)
            make_odd(second)
            make_even(second)

        run_odd(second)
        sweep(second)

    @pl.when(core == 0)
    def _():
        @pl.when(position(first) < SEND_EARLY)
        def _():
            pl.semaphore_wait(go_sem, 1)

        send_second()

    def add_own(d):
        q = position(d)

        @pl.when(q >= 1)
        def _():
            @pl.when(is_odd & (q == LAST))
            def _():
                wait_pieces(own_in.at[d], own_in_got.at[d], 7)

            @pl.when((core == 0) | ((q >= SLOW) & (q < LAST)))
            def _():
                wait_pieces(own_in.at[d], own_in_got.at[d], 8)

            solved[...] += jnp.dot(
                piece_row(own_in.at[d]), kept[d].reshape(1024, 1024), preferred_element_type=F32
            )

    add_own(first)
    add_own(second)
    out[0] = solved[...]

    sent_factors(second)

    def drain(d, count):
        part = odd_in.at[d, pl.ds(0, count)]
        remote(part, part, sent_sem.at[d], own_in_got.at[d], layer, odd_plane).wait_send()

    @pl.when(core == 0)
    def _():
        even_solved.wait_send()

        @pl.when(early == 0)
        def _():
            slow_even(sent_solved).wait_send()

        @pl.when(is_slow)
        def _():
            drain(first, 8)

    @pl.when(is_odd)
    def _():
        @pl.when((early >= 1) & (early < SLOW))
        def _():
            slow_even(slow_sent.at[0]).wait_send()
            slow_odd(slow_sent.at[1]).wait_send()

        for d in range(2):
            q = position(d)

            @pl.when(sends_solved(d))
            def _():
                odd_solved(d).wait_send()

            @pl.when((q >= SLOW) & (q < LAST))
            def _():
                drain(d, 8)

            @pl.when((q >= SLOW) & (q < LAST))
            def _():
                drain(d, 7)

            @pl.when((q == LAST) | ((q >= 1) & (q < SLOW)))
            def _():
                drain(d, 6)

            @pl.when(q >= 1)
            def _():
                relay_even(d).wait_send()

            @pl.when(q > SLOW)
            def _():
                relay_odd(d).wait_send()


def shards(*arrays):
    anywhere = pl.BlockSpec(memory_space=pl.ANY)
    scalars = pl.BlockSpec(memory_space=pltpu.SMEM)
    dma, vmem = pltpu.SemaphoreType.DMA, pltpu.VMEM
    return pl.pallas_call(
        kernel,
        name="sweep",
        out_shape=jax.ShapeDtypeStruct((1, SOURCES, 1024), F32),
        in_specs=[anywhere] * 6 + [scalars] * 2,
        out_specs=pl.BlockSpec(memory_space=pltpu.VMEM),
        scratch_shapes=[
            vmem((SOURCES, 1024), F32),
            vmem((8, 128, 128), F32),
            vmem((SOURCES, 1024), F32),
            vmem((SOURCES, 1024), BF16),
            vmem((3, SOURCES, 1024), BF16),
            vmem((2, 8, 128, 1024), BF16),
            vmem((2, 8, 128, 1024), BF16),
            vmem((2, 8, 128, 1024), BF16),
            vmem((2, 8, 128, 1024), BF16),
            vmem((2, 8, 128, 1024), BF16),
            vmem((2, CHIPS, CHIPS, 256, 256), BF16),
            vmem((2, CHIPS, CHIPS, 256, 256), BF16),
            vmem((2, CHIPS, SOURCES, 256), F32),
            vmem((2, CHIPS, SOURCES, 256), F32),
            vmem((2, 8, SOURCES, 128), BF16),
            vmem((2, 8, SOURCES, 128), BF16),
            vmem((2, 8, SOURCES, 128), BF16),
            vmem((2, 2, CHIPS, 2, SOURCES, 128), BF16),
            vmem((2, SOURCES, 1024), BF16),
            dma((6,)),
            dma((2,)),
            dma((2,)),
            dma((2,)),
            dma((2,)),
            dma((2, 2)),
            dma((2,)),
            dma((2,)),
            dma((2,)),
            dma((2, CHIPS)),
            dma(()),
            dma((2,)),
            dma((2, 2)),
            dma((2, 2)),
            dma((2,)),
            pltpu.SemaphoreType.REGULAR,
        ],
        compiler_params=pltpu.CompilerParams(
            collective_id=0, has_side_effects=True, vmem_limit_bytes=56 << 20
        ),
    )(*arrays)


def solution(mesh):
    in_specs = (
        P("layer", None, "plane"),
        P("layer", "plane", None, None),
        P("layer", None, None, "plane"),
        P("layer", None, None, "plane"),
        P("layer", None, None, "plane"),
        P("layer", None, None, "plane"),
        P("layer", None, "plane", None),
        P("layer", None, "plane", None),
    )
    return jax.shard_map(
        shards, mesh=mesh, in_specs=in_specs, out_specs=P("layer", None, "plane"), check_vma=False
    )
```

```python
import jax
import jax.numpy as jnp
from jax import lax
from jax.experimental import pallas as pl
from jax.experimental.pallas import tpu as pltpu
from jax.sharding import PartitionSpec as P

MESH = pl.DeviceIdType.MESH
BF16, F32 = jnp.bfloat16, jnp.float32
LAYERS, CHIPS, SOURCES = 32, 4, 16
LAST = LAYERS - 1
SEND_EARLY, MAKE_EARLY = 11, 14
SLOW = 3
NT = (((1,), (1,)), ((), ()))


def piece_row(ref):
    return jnp.concatenate([ref[j] for j in range(8)], axis=1)


def kernel(
    sources, fronts, down_left, down_right, up_left, up_right, ranks, pattern, out,
    src, tri, solved, solved_even, solved_odd, kept, even_right, odd_right, even_left, odd_left,
    even_step, odd_step, even_start, odd_start, even_in, pieces, sent,
    slow_sent, load_sem, kept_sem, left_sem, solved_sem, sent_sem, relay_sem, slow_sem,
    even_right_got, odd_right_got, even_left_got, solved_even_got, solved_odd_got, even_in_got, got, go_sem,
):
    layer, plane = lax.axis_index("layer"), lax.axis_index("plane")
    y, core = plane // 2, lax.rem(plane, 2)
    is_odd = core == 1
    odd_plane = 2 * y + 1
    upper = (layer >= LAYERS // 2).astype(jnp.int32)
    first, second = upper, 1 - upper
    lefts, rights = (down_left, up_left), (down_right, up_right)

    def sign(d):
        return 1 - 2 * d

    def position(d):
        return jnp.where(d == 0, layer, LAST - layer)

    def remote(source, target, send, got, to_layer, to_plane):
        return pltpu.make_async_remote_copy(
            source, target, send, got, device_id=(to_layer, to_plane), device_id_type=MESH
        )

    load_tri = pltpu.make_async_copy(fronts.at[0], tri, load_sem.at[0])
    load_src = pltpu.make_async_copy(sources.at[0], src, load_sem.at[1])
    def each(d, action):
        for way in range(2):
            pl.when(d == way)(lambda: action(way))

    def load_right(way):
        return pltpu.make_async_copy(rights[way].at[0], kept.at[way], load_sem.at[2 + way])

    def load_left(way):
        return pltpu.make_async_copy(lefts[way].at[0], odd_left.at[way], load_sem.at[4 + way])

    each(first, lambda way: load_right(way).start())
    load_tri.start()
    load_src.start()

    early = position(first)
    forward = sign(first)
    is_slow = (early >= 1) & (early <= SLOW)

    @pl.when(is_odd | is_slow)
    def _():
        each(first, lambda way: load_left(way).start())

    barrier = pltpu.get_barrier_semaphore()

    def greet(to_layer, to_plane):
        pl.semaphore_signal(barrier, inc=1, device_id=(to_layer, to_plane), device_id_type=MESH)

    def reach(r):
        return jnp.minimum(layer + r, LAST) - jnp.maximum(layer - r, 0) + 1

    @pl.when(is_odd)
    def _():
        for by in (-2, -1, 1, 2):

            @pl.when((layer + by >= 0) & (layer + by <= LAST))
            def _():
                for other in range(CHIPS):
                    greet(layer + by, 2 * other + 1)

        for turn in range(1, CHIPS):
            greet(layer, 2 * lax.rem(y + turn, CHIPS) + 1)
        for by in (-1, 0, 1):

            @pl.when((layer + by >= 0) & (layer + by <= LAST))
            def _():
                greet(layer + by, 2 * y)

        beside_slow = is_slow.astype(jnp.int32)
        past_slow = ((early >= 2) & (early <= SLOW + 1)).astype(jnp.int32)
        for turn in range(1, CHIPS):

            @pl.when(is_slow)
            def _():
                greet(layer, 2 * lax.rem(y + turn, CHIPS))

            @pl.when((early >= 2) & (early <= SLOW + 1))
            def _():
                greet(layer - forward, 2 * lax.rem(y + turn, CHIPS))

        pl.semaphore_wait(barrier, CHIPS * reach(2) - 1 + reach(1) + (CHIPS - 1) * (beside_slow + past_slow))

    @pl.when(core == 0)
    def _():
        for by in (-1, 0, 1):

            @pl.when((layer + by >= 0) & (layer + by <= LAST))
            def _():
                greet(layer + by, odd_plane)

        @pl.when(is_slow)
        def _():
            for turn in range(1, CHIPS):
                greet(layer, 2 * lax.rem(y + turn, CHIPS) + 1)
                greet(layer + forward, 2 * lax.rem(y + turn, CHIPS) + 1)

        @pl.when(early == 0)
        def _():
            greet(layer + forward, plane)

        @pl.when(early == 1)
        def _():
            greet(layer - forward, plane)

        pl.semaphore_wait(
            barrier, reach(1) + 2 * (CHIPS - 1) * is_slow.astype(jnp.int32) + (early <= 1).astype(jnp.int32)
        )

    def send_left(d):
        for way in range(2):

            @pl.when((core == 0) & (d == way) & (position(way) > SLOW))
            def _():
                for chip in range(CHIPS):
                    pair = pl.ds(2 * chip, 2)
                    remote(
                        lefts[way].at[0, pair], even_left.at[way, pair], left_sem.at[way], even_left_got.at[way, chip],
                        layer - sign(way), odd_plane,
                    ).start()

    def send_right(d):
        @pl.when(core == 0)
        def _():
            remote(kept.at[d], even_right.at[d], kept_sem.at[d], even_right_got.at[d], layer, odd_plane).start()

        @pl.when(is_odd & (position(d) >= SLOW) & (position(d) < LAST))
        def _():
            remote(
                kept.at[d], odd_right.at[d], kept_sem.at[d], odd_right_got.at[d], layer + sign(d), odd_plane
            ).start()

    def sent_factors(d):
        @pl.when((core == 0) & (position(d) > SLOW))
        def _():
            remote(even_left.at[d], even_left.at[d], left_sem.at[d], even_left_got.at[d, 0], layer, odd_plane).wait_send()

        @pl.when((core == 0) | ((position(d) >= SLOW) & (position(d) < LAST)))
        def _():
            remote(kept.at[d], even_right.at[d], kept_sem.at[d], even_right_got.at[d], layer, odd_plane).wait_send()

    def mask_right(d):
        for j in range(8):
            top = ranks[0, d, 0, j] * pattern[0, d, 0, j]
            rows = lax.broadcasted_iota(jnp.int32, (128, 1024), 0)
            kept[d, j] = jnp.where(rows < top, kept[d, j].astype(F32), 0.0).astype(BF16)

    send_left(first)
    each(first, lambda way: load_right(way).wait())
    mask_right(first)
    send_right(first)
    each(second, lambda way: load_right(way).start())

    @pl.when(is_odd)
    def _():
        each(second, lambda way: load_left(way).start())

    load_tri.wait()
    load_src.wait()
    row = lax.broadcasted_iota(jnp.int32, (128, 128), 0)
    col = lax.broadcasted_iota(jnp.int32, (128, 128), 1)

    def exact(a, b):
        return jnp.dot(a, b, preferred_element_type=F32, precision=lax.Precision.HIGHEST)

    by_col, units, inverses = [], [], []
    for b in range(8):
        block = tri[b]
        diagonal = jnp.where(row == col, block, 0.0)
        by_row = 1.0 / jnp.sum(diagonal, axis=1, keepdims=True)
        by_col.append(1.0 / jnp.sum(diagonal, axis=0, keepdims=True))
        units.append(jnp.where(row > col, block * by_row, 0.0))
        inverses.append(jnp.where(row == col, 1.0, 0.0))
    for half in (1, 2, 4, 8, 16, 32, 64):
        joins = (row // (2 * half) == col // (2 * half)) & (row // half != col // half)
        for b in range(8):
            part = jnp.where(joins, units[b], 0.0)
            if half > 1:
                part = exact(inverses[b], exact(part, inverses[b]))
            inverses[b] = inverses[b] - part
    for b in range(8):
        solved[:, 128 * b : 128 * (b + 1)] = lax.dot_general(
            src[:, 128 * b : 128 * (b + 1)] * by_col[b], inverses[b], NT,
            preferred_element_type=F32, precision=lax.Precision.HIGHEST,
        )
    sent_solved = solved_odd.at[2]
    sent_solved[...] = solved[...].astype(BF16)
    even_solved = remote(sent_solved, solved_even, solved_sem.at[0], solved_even_got, layer, odd_plane)

    def odd_solved(d):
        return remote(
            sent_solved, solved_odd.at[d], solved_sem.at[d], solved_odd_got.at[d], layer + sign(d), odd_plane
        )

    def sends_solved(d):
        return is_odd & (position(d) < LAST) & ((position(d) == 0) | (position(d) >= SLOW))

    def slow_even(source):
        return remote(source, solved_even, slow_sem.at[0], solved_even_got, layer + forward, 2 * y)

    def slow_odd(source):
        return remote(
            source, solved_odd.at[first], slow_sem.at[1], solved_odd_got.at[first], layer + forward, odd_plane
        )

    @pl.when((core == 0) & (early == 0))
    def _():
        slow_even(sent_solved).start()

    @pl.when(core == 0)
    def _():
        even_solved.start()

    for d in range(2):

        @pl.when(sends_solved(d))
        def _():
            odd_solved(d).start()

    each(second, lambda way: load_right(way).wait())
    mask_right(second)

    def send_second():
        sent_factors(first)
        send_left(second)
        send_right(second)

    def open_way(d):
        each(d, lambda way: load_left(way).wait())

        @pl.when(position(d) >= 1)
        def _():
            remote(sent_solved, solved_odd.at[d], solved_sem.at[d], solved_odd_got.at[d], layer, odd_plane).wait_recv()
            begin = lax.dot_general(
                solved_odd[d], odd_left[d].reshape(1024, 1024), NT, preferred_element_type=F32
            )
            for chip in range(CHIPS):
                odd_start[d, chip] = begin[:, 256 * chip : 256 * (chip + 1)]

    def wait_even_right(d):
        remote(kept.at[d], even_right.at[d], kept_sem.at[d], even_right_got.at[d], layer, odd_plane).wait_recv()

    def make(right, left, d, chip, step):
        block = left[d, pl.ds(2 * chip, 2)].reshape(256, 1024)
        full = right[d].reshape(1024, 1024)
        columns = lax.dot_general(full, block, NT, preferred_element_type=F32).astype(BF16)
        step[d, chip] = columns.reshape(CHIPS, 256, 256)

    def wait_odd_right(d):
        remote(kept.at[d], odd_right.at[d], kept_sem.at[d], odd_right_got.at[d], layer, odd_plane).wait_recv()

    def make_odd(d):
        @pl.when(position(d) > SLOW)
        def _():
            wait_odd_right(d)

            @pl.loop(0, CHIPS)
            def _(chip):
                make(odd_right, odd_left, d, chip, odd_step)

    def wait_even_left(d, chip):
        part = even_left.at[d, pl.ds(2 * chip, 2)]
        remote(part, part, left_sem.at[d], even_left_got.at[d, chip], layer, odd_plane).wait_recv()

    def make_even(d):
        @pl.when((position(d) > SLOW + 1) & (position(d) < LAST))
        def _():
            @pl.loop(0, CHIPS)
            def _(chip):
                wait_even_left(d, chip)
                block = even_left[d, pl.ds(2 * chip, 2)].reshape(256, 1024)
                even_start[d, chip] = lax.dot_general(solved_even[...], block, NT, preferred_element_type=F32)
                make(even_right, even_left, d, chip, even_step)

    def wait_pieces(ref, got, count):
        remote(ref.at[pl.ds(0, count)], ref.at[pl.ds(0, count)], sent_sem.at[0], got, layer, odd_plane).wait_recv()

    def pair_row(ref, chip):
        return jnp.concatenate([ref[2 * chip], ref[2 * chip + 1]], axis=1)

    def start_only(d, start, deliver):
        for turn in (2, 1, 3, 0):
            other = lax.rem(y + turn, CHIPS)
            deliver(turn, other, start[d, other].astype(BF16))

    def advance(d, ref, got_near, got_far, near, step, start, deliver):
        turns = (2, 1, 3, 0)
        others = {turn: lax.rem(y + turn, CHIPS) for turn in turns}
        wait_pieces(ref, got_near, near)
        totals = {turn: start[d, others[turn]] for turn in turns}
        for source in (0, 1, 3):
            values = pair_row(ref, others[source])
            for turn in turns:
                totals[turn] += jnp.dot(
                    values, step[d, others[turn], others[source]], preferred_element_type=F32
                )
        wait_pieces(ref, got_far, 2)
        values = pair_row(ref, others[2])
        for turn in turns:
            total = totals[turn] + jnp.dot(values, step[d, others[turn], others[2]], preferred_element_type=F32)
            deliver(turn, others[turn], total.astype(BF16))

    def far(turn):
        return 1 if turn == 2 else 0

    def odd_deliver(d):
        q = position(d)
        direct = (q == LAST) | (q < SLOW)
        kind = direct.astype(jnp.int32)
        odd_layer = layer + (1 - kind) * sign(d)

        def deliver(turn, other, result):
            for part in range(2):
                sent[d, 1, other, part] = result[:, 128 * part : 128 * (part + 1)]
            if turn == 0:
                even_in[d, odd_plane] = result[:, :128]
            else:
                remote(
                    sent.at[d, 1, other, 0], even_in.at[d, odd_plane], sent_sem.at[d], even_in_got.at[d, far(turn)],
                    layer, 2 * other + 1,
                ).start()

            odd_part = remote(
                sent.at[d, 1, other, 1], pieces.at[kind, d, odd_plane], sent_sem.at[d], got.at[kind, d, far(turn)],
                odd_layer, 2 * other + 1,
            )
            if turn != 0:
                odd_part.start()
            else:
                pl.when(jnp.logical_not(direct))(odd_part.start)

                @pl.when(direct)
                def _():
                    pieces[1, d, odd_plane] = result[:, 128:]

        return deliver

    def run_odd(d):
        @pl.when(position(d) > SLOW)
        def _():
            advance(d, pieces.at[0, d], got.at[0, d, 0], got.at[0, d, 1], 6, odd_step, odd_start, odd_deliver(d))

    def even_deliver(d):
        kind = (position(d) == LAST - 1).astype(jnp.int32)

        def deliver(turn, other, result):
            for part in range(2):
                sent[d, 0, other, part] = result[:, 128 * part : 128 * (part + 1)]
            remote(
                sent.at[d, 0, other, 0], even_in.at[d, 2 * y], sent_sem.at[d], even_in_got.at[d, far(turn)],
                layer + sign(d), 2 * other + 1,
            ).start()

            remote(
                sent.at[d, 0, other, 1], pieces.at[kind, d, 2 * y], sent_sem.at[d], got.at[kind, d, far(turn)],
                layer + (2 - kind) * sign(d), 2 * other + 1,
            ).start()

        return deliver

    def run_even(d):
        q = position(d)

        @pl.when((q > SLOW + 1) & (q < LAST))
        def _():
            advance(
                d, even_in.at[d], even_in_got.at[d, 0], even_in_got.at[d, 1], 5, even_step, even_start,
                even_deliver(d),
            )

        @pl.when(q == LAST)
        def _():
            wait_pieces(even_in.at[d], even_in_got.at[d, 0], 5)
            wait_pieces(even_in.at[d], even_in_got.at[d, 1], 2)

    def slow_deliver(turn, other, result):
        for part in range(2):
            sent[first, 0, other, part] = result[:, 128 * part : 128 * (part + 1)]
        remote(
            sent.at[first, 0, other, 0], even_in.at[first, 2 * y], sent_sem.at[first],
            even_in_got.at[first, far(turn)], layer, 2 * other + 1,
        ).start()

        kind = (early < SLOW).astype(jnp.int32)
        remote(
            sent.at[first, 0, other, 1], pieces.at[kind, first, 2 * y], sent_sem.at[first],
            got.at[kind, first, far(turn)], layer + (1 - kind) * forward, 2 * other + 1,
        ).start()

    @pl.when((core == 0) & is_slow)
    def _():
        each(first, lambda way: load_left(way).wait())
        remote(sent_solved, solved_even, solved_sem.at[0], solved_even_got, layer, 2 * y).wait_recv()
        for turn in (2, 1, 3, 0):
            other = lax.rem(y + turn, CHIPS)
            block = odd_left[first, pl.ds(2 * other, 2)].reshape(256, 1024)
            result = lax.dot_general(solved_even[...], block, NT, preferred_element_type=F32)
            slow_deliver(turn, other, result.astype(BF16))

    def join(ref, right, left, part, deliver):
        trace = jnp.dot(piece_row(ref), right[first].reshape(1024, 1024), preferred_element_type=F32)
        whole = (part.astype(F32) + trace).astype(BF16)
        for turn in (2, 1, 3, 0):
            other = lax.rem(y + turn, CHIPS)
            block = left[first, pl.ds(2 * other, 2)].reshape(256, 1024)
            deliver(turn, other, lax.dot_general(whole, block, NT, preferred_element_type=F32).astype(BF16))

    def join_odd():
        wait_odd_right(first)
        wait_pieces(pieces.at[0, first], got.at[0, first, 0], 6)
        wait_pieces(pieces.at[0, first], got.at[0, first, 1], 2)
        join(pieces.at[0, first], odd_right, odd_left, solved_odd[first], odd_deliver(first))

    def join_even():
        for chip in range(CHIPS):
            wait_even_left(first, chip)
        wait_pieces(even_in.at[first], even_in_got.at[first, 0], 5)
        wait_pieces(even_in.at[first], even_in_got.at[first, 1], 2)
        join(even_in.at[first], even_right, even_left, solved_even[...], even_deliver(first))

    def slow_step():
        wait_pieces(even_in.at[first], even_in_got.at[first, 0], 5)
        wait_pieces(even_in.at[first], even_in_got.at[first, 1], 2)
        trace = jnp.dot(
            piece_row(even_in.at[first]), even_right[first].reshape(1024, 1024), preferred_element_type=F32
        )
        slow_sent[0] = (solved_even[...].astype(F32) + trace).astype(BF16)
        slow_even(slow_sent.at[0]).start()
        wait_pieces(pieces.at[1, first], got.at[1, first, 0], 5)
        wait_pieces(pieces.at[1, first], got.at[1, first, 1], 2)
        trace = jnp.dot(
            piece_row(pieces.at[1, first]), kept[first].reshape(1024, 1024), preferred_element_type=F32
        )
        slow_sent[1] = (solved[...] + trace).astype(BF16)
        slow_odd(slow_sent.at[1]).start()

    def relay_even(d):
        return remote(even_in.at[d], pieces.at[1, d], relay_sem.at[0, d], got.at[1, d, 0], layer, 2 * y)

    def relay_odd(d):
        return remote(pieces.at[0, d], pieces.at[1, d], relay_sem.at[1, d], got.at[1, d, 0], layer - sign(d), odd_plane)

    def sweep(d):
        q = position(d)
        run_even(d)

        @pl.when(q >= 1)
        def _():
            relay_even(d).start()

        @pl.when(q > SLOW)
        def _():
            relay_odd(d).start()

    @pl.when(is_odd)
    def _():
        remote(sent_solved, solved_even, solved_sem.at[0], solved_even_got, layer, odd_plane).wait_recv()
        wait_even_right(first)
        open_way(first)

        @pl.when(is_slow)
        def _():
            start_only(first, odd_start, odd_deliver(first))

        @pl.when((early >= 1) & (early < SLOW))
        def _():
            slow_step()

        @pl.when(position(first) >= SEND_EARLY)
        def _():
            send_second()

        @pl.when(early == SLOW + 1)
        def _():
            join_odd()

        @pl.when((early == SLOW) | (early == SLOW + 1))
        def _():
            join_even()

        @pl.when(early > SLOW + 1)
        def _():
            make_odd(first)

        make_even(first)

        @pl.when(position(first) >= MAKE_EARLY)
        def _():
            wait_even_right(second)
            open_way(second)
            make_odd(second)
            make_even(second)

        @pl.when(early > SLOW + 1)
        def _():
            run_odd(first)

        sweep(first)

        @pl.when(position(first) < SEND_EARLY)
        def _():
            pl.semaphore_signal(go_sem, inc=1, device_id=(layer, 2 * y), device_id_type=MESH)
            send_second()

        @pl.when(position(first) < MAKE_EARLY)
        def _():
            wait_even_right(second)
            open_way(second)
            make_odd(second)
            make_even(second)

        run_odd(second)
        sweep(second)

    @pl.when(core == 0)
    def _():
        @pl.when(position(first) < SEND_EARLY)
        def _():
            pl.semaphore_wait(go_sem, 1)

        send_second()

    def add_own(d):
        q = position(d)

        @pl.when(q >= 1)
        def _():
            @pl.when(is_odd & (q == LAST))
            def _():
                wait_pieces(pieces.at[1, d], got.at[1, d, 0], 5)
                wait_pieces(pieces.at[1, d], got.at[1, d, 1], 2)

            @pl.when((core == 0) | ((q >= SLOW) & (q < LAST)))
            def _():
                wait_pieces(pieces.at[1, d], got.at[1, d, 0], 8)

            solved[...] += jnp.dot(
                piece_row(pieces.at[1, d]), kept[d].reshape(1024, 1024), preferred_element_type=F32
            )

    add_own(first)
    add_own(second)
    out[0] = solved[...]

    sent_factors(second)

    def drain(d, count):
        part = pieces.at[0, d, pl.ds(0, count)]
        remote(part, part, sent_sem.at[d], got.at[1, d, 0], layer, odd_plane).wait_send()

    @pl.when(core == 0)
    def _():
        even_solved.wait_send()

        @pl.when(early == 0)
        def _():
            slow_even(sent_solved).wait_send()

        @pl.when(is_slow)
        def _():
            drain(first, 8)

    @pl.when(is_odd)
    def _():
        @pl.when((early >= 1) & (early < SLOW))
        def _():
            slow_even(slow_sent.at[0]).wait_send()
            slow_odd(slow_sent.at[1]).wait_send()

        for d in range(2):
            q = position(d)

            @pl.when(sends_solved(d))
            def _():
                odd_solved(d).wait_send()

            @pl.when((q >= SLOW) & (q < LAST))
            def _():
                drain(d, 8)

            @pl.when((q >= SLOW) & (q < LAST))
            def _():
                drain(d, 7)

            @pl.when((q == LAST) | ((q >= 1) & (q < SLOW)))
            def _():
                drain(d, 6)

            @pl.when(q >= 1)
            def _():
                relay_even(d).wait_send()

            @pl.when(q > SLOW)
            def _():
                relay_odd(d).wait_send()


def shards(*arrays):
    anywhere = pl.BlockSpec(memory_space=pl.ANY)
    scalars = pl.BlockSpec(memory_space=pltpu.SMEM)
    dma, vmem = pltpu.SemaphoreType.DMA, pltpu.VMEM
    return pl.pallas_call(
        kernel,
        name="sweep",
        out_shape=jax.ShapeDtypeStruct((1, SOURCES, 1024), F32),
        in_specs=[anywhere] * 6 + [scalars] * 2,
        out_specs=pl.BlockSpec(memory_space=pltpu.VMEM),
        scratch_shapes=[
            vmem((SOURCES, 1024), F32),
            vmem((8, 128, 128), F32),
            vmem((SOURCES, 1024), F32),
            vmem((SOURCES, 1024), BF16),
            vmem((3, SOURCES, 1024), BF16),
            vmem((2, 8, 128, 1024), BF16),
            vmem((2, 8, 128, 1024), BF16),
            vmem((2, 8, 128, 1024), BF16),
            vmem((2, 8, 128, 1024), BF16),
            vmem((2, 8, 128, 1024), BF16),
            vmem((2, CHIPS, CHIPS, 256, 256), BF16),
            vmem((2, CHIPS, CHIPS, 256, 256), BF16),
            vmem((2, CHIPS, SOURCES, 256), F32),
            vmem((2, CHIPS, SOURCES, 256), F32),
            vmem((2, 8, SOURCES, 128), BF16),
            vmem((2, 2, 8, SOURCES, 128), BF16),
            vmem((2, 2, CHIPS, 2, SOURCES, 128), BF16),
            vmem((2, SOURCES, 1024), BF16),
            dma((6,)),
            dma((2,)),
            dma((2,)),
            dma((2,)),
            dma((2,)),
            dma((2, 2)),
            dma((2,)),
            dma((2,)),
            dma((2,)),
            dma((2, CHIPS)),
            dma(()),
            dma((2,)),
            dma((2, 2)),
            dma((2, 2, 2)),
            pltpu.SemaphoreType.REGULAR,
        ],
        compiler_params=pltpu.CompilerParams(
            collective_id=0, has_side_effects=True, vmem_limit_bytes=56 << 20
        ),
    )(*arrays)


def solution(mesh):
    in_specs = (
        P("layer", None, "plane"),
        P("layer", "plane", None, None),
        P("layer", None, None, "plane"),
        P("layer", None, None, "plane"),
        P("layer", None, None, "plane"),
        P("layer", None, None, "plane"),
        P("layer", None, "plane", None),
        P("layer", None, "plane", None),
    )
    return jax.shard_map(
        shards, mesh=mesh, in_specs=in_specs, out_specs=P("layer", None, "plane"), check_vma=False
    )
```

```python
import jax
import jax.numpy as jnp
from jax import lax
from jax.experimental import pallas as pl
from jax.experimental.pallas import tpu as pltpu
from jax.sharding import PartitionSpec as P

MESH = pl.DeviceIdType.MESH
BF16, F32 = jnp.bfloat16, jnp.float32
LAYERS, CHIPS, SOURCES = 32, 4, 16
LAST = LAYERS - 1
SEND_EARLY, MAKE_EARLY = 11, 14
SLOW = 3
NT = (((1,), (1,)), ((), ()))


def piece_row(ref):
    return jnp.concatenate([ref[j] for j in range(8)], axis=1)


def kernel(
    sources, fronts, down_left, down_right, up_left, up_right, ranks, pattern, out,
    src, tri, solved, solved_even, solved_odd, kept, even_right, odd_right, even_left, odd_left,
    even_step, odd_step, even_start, odd_start, even_in, pieces, sent,
    slow_sent, load_sem, kept_sem, left_sem, solved_sem, sent_sem, relay_sem, slow_sem,
    even_right_got, odd_right_got, even_left_got, solved_even_got, solved_odd_got, even_in_got, got, go_sem,
):
    layer, plane = lax.axis_index("layer"), lax.axis_index("plane")
    y, core = plane // 2, lax.rem(plane, 2)
    is_odd = core == 1
    odd_plane = 2 * y + 1
    upper = (layer >= LAYERS // 2).astype(jnp.int32)
    first, second = upper, 1 - upper
    lefts, rights = (down_left, up_left), (down_right, up_right)

    def sign(d):
        return 1 - 2 * d

    def position(d):
        return jnp.where(d == 0, layer, LAST - layer)

    def remote(source, target, send, got, to_layer, to_plane):
        return pltpu.make_async_remote_copy(
            source, target, send, got, device_id=(to_layer, to_plane), device_id_type=MESH
        )

    load_tri = pltpu.make_async_copy(fronts.at[0], tri, load_sem.at[0])
    load_src = pltpu.make_async_copy(sources.at[0], src, load_sem.at[1])
    def each(d, action):
        for way in range(2):
            pl.when(d == way)(lambda: action(way))

    def load_right(way):
        return pltpu.make_async_copy(rights[way].at[0], kept.at[way], load_sem.at[2 + way])

    def load_left(way):
        return pltpu.make_async_copy(lefts[way].at[0], odd_left.at[way], load_sem.at[4 + way])

    each(first, lambda way: load_right(way).start())
    load_tri.start()
    load_src.start()

    early = position(first)
    forward = sign(first)
    is_slow = (early >= 1) & (early <= SLOW)

    @pl.when(is_odd | is_slow)
    def _():
        each(first, lambda way: load_left(way).start())

    barrier = pltpu.get_barrier_semaphore()

    def greet(to_layer, to_plane):
        pl.semaphore_signal(barrier, inc=1, device_id=(to_layer, to_plane), device_id_type=MESH)

    def reach(r):
        return jnp.minimum(layer + r, LAST) - jnp.maximum(layer - r, 0) + 1

    @pl.when(is_odd)
    def _():
        for by in (-2, -1, 1, 2):

            @pl.when((layer + by >= 0) & (layer + by <= LAST))
            def _():
                for other in range(CHIPS):
                    greet(layer + by, 2 * other + 1)

        for turn in range(1, CHIPS):
            greet(layer, 2 * lax.rem(y + turn, CHIPS) + 1)
        for by in (-1, 0, 1):

            @pl.when((layer + by >= 0) & (layer + by <= LAST))
            def _():
                greet(layer + by, 2 * y)

        beside_slow = is_slow.astype(jnp.int32)
        past_slow = ((early >= 2) & (early <= SLOW + 1)).astype(jnp.int32)
        for turn in range(1, CHIPS):

            @pl.when(is_slow)
            def _():
                greet(layer, 2 * lax.rem(y + turn, CHIPS))

            @pl.when((early >= 2) & (early <= SLOW + 1))
            def _():
                greet(layer - forward, 2 * lax.rem(y + turn, CHIPS))

        pl.semaphore_wait(barrier, CHIPS * reach(2) - 1 + reach(1) + (CHIPS - 1) * (beside_slow + past_slow))

    @pl.when(core == 0)
    def _():
        for by in (-1, 0, 1):

            @pl.when((layer + by >= 0) & (layer + by <= LAST))
            def _():
                greet(layer + by, odd_plane)

        @pl.when(is_slow)
        def _():
            for turn in range(1, CHIPS):
                greet(layer, 2 * lax.rem(y + turn, CHIPS) + 1)
                greet(layer + forward, 2 * lax.rem(y + turn, CHIPS) + 1)

        @pl.when(early == 0)
        def _():
            greet(layer + forward, plane)

        @pl.when(early == 1)
        def _():
            greet(layer - forward, plane)

        pl.semaphore_wait(
            barrier, reach(1) + 2 * (CHIPS - 1) * is_slow.astype(jnp.int32) + (early <= 1).astype(jnp.int32)
        )

    def send_left(d):
        for way in range(2):

            @pl.when((core == 0) & (d == way) & (position(way) > SLOW))
            def _():
                for chip in range(CHIPS):
                    pair = pl.ds(2 * chip, 2)
                    remote(
                        lefts[way].at[0, pair], even_left.at[way, pair], left_sem.at[way], even_left_got.at[way, chip],
                        layer - sign(way), odd_plane,
                    ).start()

    def send_right(d):
        @pl.when(core == 0)
        def _():
            remote(kept.at[d], even_right.at[d], kept_sem.at[d], even_right_got.at[d], layer, odd_plane).start()

        @pl.when(is_odd & (position(d) >= SLOW) & (position(d) < LAST))
        def _():
            remote(
                kept.at[d], odd_right.at[d], kept_sem.at[d], odd_right_got.at[d], layer + sign(d), odd_plane
            ).start()

    def sent_factors(d):
        @pl.when((core == 0) & (position(d) > SLOW))
        def _():
            remote(even_left.at[d], even_left.at[d], left_sem.at[d], even_left_got.at[d, 0], layer, odd_plane).wait_send()

        @pl.when((core == 0) | ((position(d) >= SLOW) & (position(d) < LAST)))
        def _():
            remote(kept.at[d], even_right.at[d], kept_sem.at[d], even_right_got.at[d], layer, odd_plane).wait_send()

    def mask_right(d):
        for j in range(8):
            top = ranks[0, d, 0, j] * pattern[0, d, 0, j]
            rows = lax.broadcasted_iota(jnp.int32, (128, 1024), 0)
            kept[d, j] = jnp.where(rows < top, kept[d, j].astype(F32), 0.0).astype(BF16)

    send_left(first)
    each(first, lambda way: load_right(way).wait())
    mask_right(first)
    send_right(first)
    each(second, lambda way: load_right(way).start())

    @pl.when(is_odd)
    def _():
        each(second, lambda way: load_left(way).start())

    load_tri.wait()
    load_src.wait()
    row = lax.broadcasted_iota(jnp.int32, (128, 128), 0)
    col = lax.broadcasted_iota(jnp.int32, (128, 128), 1)

    def exact(a, b):
        return jnp.dot(a, b, preferred_element_type=F32, precision=lax.Precision.HIGHEST)

    by_col, units, inverses = [], [], []
    for b in range(8):
        block = tri[b]
        diagonal = jnp.where(row == col, block, 0.0)
        by_row = 1.0 / jnp.sum(diagonal, axis=1, keepdims=True)
        by_col.append(1.0 / jnp.sum(diagonal, axis=0, keepdims=True))
        units.append(jnp.where(row > col, block * by_row, 0.0))
        inverses.append(jnp.where(row == col, 1.0, 0.0))
    for half in (1, 2, 4, 8, 16, 32, 64):
        joins = (row // (2 * half) == col // (2 * half)) & (row // half != col // half)
        for b in range(8):
            part = jnp.where(joins, units[b], 0.0)
            if half > 1:
                part = exact(inverses[b], exact(part, inverses[b]))
            inverses[b] = inverses[b] - part
    for b in range(8):
        solved[:, 128 * b : 128 * (b + 1)] = lax.dot_general(
            src[:, 128 * b : 128 * (b + 1)] * by_col[b], inverses[b], NT,
            preferred_element_type=F32, precision=lax.Precision.HIGHEST,
        )
    sent_solved = solved_odd.at[2]
    sent_solved[...] = solved[...].astype(BF16)
    even_solved = remote(sent_solved, solved_even, solved_sem.at[0], solved_even_got, layer, odd_plane)

    def odd_solved(d):
        return remote(
            sent_solved, solved_odd.at[d], solved_sem.at[d], solved_odd_got.at[d], layer + sign(d), odd_plane
        )

    def sends_solved(d):
        return is_odd & (position(d) < LAST) & ((position(d) == 0) | (position(d) >= SLOW))

    def slow_even(source):
        return remote(source, solved_even, slow_sem.at[0], solved_even_got, layer + forward, 2 * y)

    def slow_odd(source):
        return remote(
            source, solved_odd.at[first], slow_sem.at[1], solved_odd_got.at[first], layer + forward, odd_plane
        )

    @pl.when((core == 0) & (early == 0))
    def _():
        slow_even(sent_solved).start()

    @pl.when(core == 0)
    def _():
        even_solved.start()

    for d in range(2):

        @pl.when(sends_solved(d))
        def _():
            odd_solved(d).start()

    each(second, lambda way: load_right(way).wait())
    mask_right(second)

    def send_second():
        sent_factors(first)
        send_left(second)
        send_right(second)

    def open_way(d):
        each(d, lambda way: load_left(way).wait())

        @pl.when(position(d) >= 1)
        def _():
            remote(sent_solved, solved_odd.at[d], solved_sem.at[d], solved_odd_got.at[d], layer, odd_plane).wait_recv()
            begin = lax.dot_general(
                solved_odd[d], odd_left[d].reshape(1024, 1024), NT, preferred_element_type=F32
            )
            for chip in range(CHIPS):
                odd_start[d, chip] = begin[:, 256 * chip : 256 * (chip + 1)]

    def wait_even_right(d):
        remote(kept.at[d], even_right.at[d], kept_sem.at[d], even_right_got.at[d], layer, odd_plane).wait_recv()

    def make(right, left, d, chip, step):
        block = left[d, pl.ds(2 * chip, 2)].reshape(256, 1024)
        full = right[d].reshape(1024, 1024)
        columns = lax.dot_general(full, block, NT, preferred_element_type=F32).astype(BF16)
        step[d, chip] = columns.reshape(CHIPS, 256, 256)

    def wait_odd_right(d):
        remote(kept.at[d], odd_right.at[d], kept_sem.at[d], odd_right_got.at[d], layer, odd_plane).wait_recv()

    def make_odd(d):
        @pl.when(position(d) > SLOW)
        def _():
            wait_odd_right(d)

            @pl.loop(0, CHIPS)
            def _(chip):
                make(odd_right, odd_left, d, chip, odd_step)

    def wait_even_left(d, chip):
        part = even_left.at[d, pl.ds(2 * chip, 2)]
        remote(part, part, left_sem.at[d], even_left_got.at[d, chip], layer, odd_plane).wait_recv()

    def make_even(d):
        @pl.when((position(d) > SLOW + 1) & (position(d) < LAST))
        def _():
            @pl.loop(0, CHIPS)
            def _(chip):
                wait_even_left(d, chip)
                block = even_left[d, pl.ds(2 * chip, 2)].reshape(256, 1024)
                even_start[d, chip] = lax.dot_general(solved_even[...], block, NT, preferred_element_type=F32)
                make(even_right, even_left, d, chip, even_step)

    def wait_pieces(ref, got, count):
        remote(ref.at[pl.ds(0, count)], ref.at[pl.ds(0, count)], sent_sem.at[0], got, layer, odd_plane).wait_recv()

    def pair_row(ref, chip):
        return jnp.concatenate([ref[2 * chip], ref[2 * chip + 1]], axis=1)

    def start_only(d, start, deliver):
        for turn in (2, 1, 3, 0):
            other = lax.rem(y + turn, CHIPS)
            deliver(turn, other, start[d, other].astype(BF16))

    last_y, first_y = (y == CHIPS - 1).astype(jnp.int32), (y == 0).astype(jnp.int32)
    comes = (0, 1 + 2 * last_y, 3 - last_y, 2 - last_y)
    goes = (2 + first_y, 1 + first_y, 3 - 2 * first_y, 0)

    def chip_at(turn):
        return lax.rem(y + turn, CHIPS)

    def seen(turn):
        return lax.rem(CHIPS - turn, CHIPS)

    def wait_from(ref, got, turn, count):
        wait_pieces(ref, got.at[turn], count)

    def wait_all(ref, got, own):
        for turn in range(CHIPS):
            wait_from(ref, got, turn, own if turn == 0 else 2)

    def advance(d, ref, got, own, step, start, deliver):
        totals = [start[d, chip_at(turn)] for turn in goes]
        for at, source in enumerate(comes):
            if at != 1:
                wait_from(ref, got, source, own if at == 0 else 2)
            if at == 0:
                wait_from(ref, got, comes[1], 2)
            values = pair_row(ref, chip_at(source))
            for index, turn in enumerate(goes):
                totals[index] += jnp.dot(
                    values, step[d, chip_at(turn), chip_at(source)], preferred_element_type=F32
                )
                if at == CHIPS - 1:
                    deliver(turn, chip_at(turn), totals[index].astype(BF16))

    def odd_deliver(d):
        q = position(d)
        direct = (q == LAST) | (q < SLOW)
        kind = direct.astype(jnp.int32)
        odd_layer = layer + (1 - kind) * sign(d)

        def deliver(turn, other, result):
            for part in range(2):
                sent[d, 1, other, part] = result[:, 128 * part : 128 * (part + 1)]
            if isinstance(turn, int) and turn == 0:
                even_in[d, odd_plane] = result[:, :128]
            else:
                remote(
                    sent.at[d, 1, other, 0], even_in.at[d, odd_plane], sent_sem.at[d], even_in_got.at[d, seen(turn)],
                    layer, 2 * other + 1,
                ).start()

            odd_part = remote(
                sent.at[d, 1, other, 1], pieces.at[kind, d, odd_plane], sent_sem.at[d], got.at[kind, d, seen(turn)],
                odd_layer, 2 * other + 1,
            )
            if not isinstance(turn, int) or turn != 0:
                odd_part.start()
            else:
                pl.when(jnp.logical_not(direct))(odd_part.start)

                @pl.when(direct)
                def _():
                    pieces[1, d, odd_plane] = result[:, 128:]

        return deliver

    def run_odd(d):
        @pl.when(position(d) > SLOW)
        def _():
            advance(d, pieces.at[0, d], got.at[0, d], 2, odd_step, odd_start, odd_deliver(d))

    def even_deliver(d):
        kind = (position(d) == LAST - 1).astype(jnp.int32)

        def deliver(turn, other, result):
            for part in range(2):
                sent[d, 0, other, part] = result[:, 128 * part : 128 * (part + 1)]
            remote(
                sent.at[d, 0, other, 0], even_in.at[d, 2 * y], sent_sem.at[d], even_in_got.at[d, seen(turn)],
                layer + sign(d), 2 * other + 1,
            ).start()

            remote(
                sent.at[d, 0, other, 1], pieces.at[kind, d, 2 * y], sent_sem.at[d], got.at[kind, d, seen(turn)],
                layer + (2 - kind) * sign(d), 2 * other + 1,
            ).start()

        return deliver

    def run_even(d):
        q = position(d)

        @pl.when((q > SLOW + 1) & (q < LAST))
        def _():
            advance(
                d, even_in.at[d], even_in_got.at[d], 1, even_step, even_start,
                even_deliver(d),
            )

        @pl.when(q == LAST)
        def _():
            wait_all(even_in.at[d], even_in_got.at[d], 1)

    def slow_deliver(turn, other, result):
        for part in range(2):
            sent[first, 0, other, part] = result[:, 128 * part : 128 * (part + 1)]
        remote(
            sent.at[first, 0, other, 0], even_in.at[first, 2 * y], sent_sem.at[first],
            even_in_got.at[first, seen(turn)], layer, 2 * other + 1,
        ).start()

        kind = (early < SLOW).astype(jnp.int32)
        remote(
            sent.at[first, 0, other, 1], pieces.at[kind, first, 2 * y], sent_sem.at[first],
            got.at[kind, first, seen(turn)], layer + (1 - kind) * forward, 2 * other + 1,
        ).start()

    @pl.when((core == 0) & is_slow)
    def _():
        each(first, lambda way: load_left(way).wait())
        remote(sent_solved, solved_even, solved_sem.at[0], solved_even_got, layer, 2 * y).wait_recv()
        for turn in (2, 1, 3, 0):
            other = lax.rem(y + turn, CHIPS)
            block = odd_left[first, pl.ds(2 * other, 2)].reshape(256, 1024)
            result = lax.dot_general(solved_even[...], block, NT, preferred_element_type=F32)
            slow_deliver(turn, other, result.astype(BF16))

    def join(ref, right, left, part, deliver):
        trace = jnp.dot(piece_row(ref), right[first].reshape(1024, 1024), preferred_element_type=F32)
        whole = (part.astype(F32) + trace).astype(BF16)
        for turn in (2, 1, 3, 0):
            other = lax.rem(y + turn, CHIPS)
            block = left[first, pl.ds(2 * other, 2)].reshape(256, 1024)
            deliver(turn, other, lax.dot_general(whole, block, NT, preferred_element_type=F32).astype(BF16))

    def join_odd():
        wait_odd_right(first)
        wait_all(pieces.at[0, first], got.at[0, first], 2)
        join(pieces.at[0, first], odd_right, odd_left, solved_odd[first], odd_deliver(first))

    def join_even():
        for chip in range(CHIPS):
            wait_even_left(first, chip)
        wait_all(even_in.at[first], even_in_got.at[first], 1)
        join(even_in.at[first], even_right, even_left, solved_even[...], even_deliver(first))

    def slow_step():
        wait_all(even_in.at[first], even_in_got.at[first], 1)
        trace = jnp.dot(
            piece_row(even_in.at[first]), even_right[first].reshape(1024, 1024), preferred_element_type=F32
        )
        slow_sent[0] = (solved_even[...].astype(F32) + trace).astype(BF16)
        slow_even(slow_sent.at[0]).start()
        wait_all(pieces.at[1, first], got.at[1, first], 1)
        trace = jnp.dot(
            piece_row(pieces.at[1, first]), kept[first].reshape(1024, 1024), preferred_element_type=F32
        )
        slow_sent[1] = (solved[...] + trace).astype(BF16)
        slow_odd(slow_sent.at[1]).start()

    def relay_even(d):
        return remote(even_in.at[d], pieces.at[1, d], relay_sem.at[0, d], got.at[1, d, 0], layer, 2 * y)

    def relay_odd(d):
        return remote(pieces.at[0, d], pieces.at[1, d], relay_sem.at[1, d], got.at[1, d, 0], layer - sign(d), odd_plane)

    def sweep(d):
        q = position(d)
        run_even(d)

        @pl.when(q >= 1)
        def _():
            relay_even(d).start()

        @pl.when(q > SLOW)
        def _():
            relay_odd(d).start()

    @pl.when(is_odd)
    def _():
        remote(sent_solved, solved_even, solved_sem.at[0], solved_even_got, layer, odd_plane).wait_recv()
        wait_even_right(first)
        open_way(first)

        @pl.when(is_slow)
        def _():
            start_only(first, odd_start, odd_deliver(first))

        @pl.when((early >= 1) & (early < SLOW))
        def _():
            slow_step()

        @pl.when(position(first) >= SEND_EARLY)
        def _():
            send_second()

        @pl.when(early == SLOW + 1)
        def _():
            join_odd()

        @pl.when((early == SLOW) | (early == SLOW + 1))
        def _():
            join_even()

        @pl.when(early > SLOW + 1)
        def _():
            make_odd(first)

        make_even(first)

        @pl.when(position(first) >= MAKE_EARLY)
        def _():
            wait_even_right(second)
            open_way(second)
            make_odd(second)
            make_even(second)

        @pl.when(early > SLOW + 1)
        def _():
            run_odd(first)

        sweep(first)

        @pl.when(position(first) < SEND_EARLY)
        def _():
            pl.semaphore_signal(go_sem, inc=1, device_id=(layer, 2 * y), device_id_type=MESH)
            send_second()

        @pl.when(position(first) < MAKE_EARLY)
        def _():
            wait_even_right(second)
            open_way(second)
            make_odd(second)
            make_even(second)

        run_odd(second)
        sweep(second)

    @pl.when(core == 0)
    def _():
        @pl.when(position(first) < SEND_EARLY)
        def _():
            pl.semaphore_wait(go_sem, 1)

        send_second()

    def add_own(d):
        q = position(d)

        @pl.when(q >= 1)
        def _():
            @pl.when(is_odd & (q == LAST))
            def _():
                wait_all(pieces.at[1, d], got.at[1, d], 1)

            @pl.when((core == 0) | ((q >= SLOW) & (q < LAST)))
            def _():
                wait_pieces(pieces.at[1, d], got.at[1, d, 0], 8)

            solved[...] += jnp.dot(
                piece_row(pieces.at[1, d]), kept[d].reshape(1024, 1024), preferred_element_type=F32
            )

    add_own(first)
    add_own(second)
    out[0] = solved[...]

    sent_factors(second)

    def drain(d, count):
        part = pieces.at[0, d, pl.ds(0, count)]
        remote(part, part, sent_sem.at[d], got.at[1, d, 0], layer, odd_plane).wait_send()

    @pl.when(core == 0)
    def _():
        even_solved.wait_send()

        @pl.when(early == 0)
        def _():
            slow_even(sent_solved).wait_send()

        @pl.when(is_slow)
        def _():
            drain(first, 8)

    @pl.when(is_odd)
    def _():
        @pl.when((early >= 1) & (early < SLOW))
        def _():
            slow_even(slow_sent.at[0]).wait_send()
            slow_odd(slow_sent.at[1]).wait_send()

        for d in range(2):
            q = position(d)

            @pl.when(sends_solved(d))
            def _():
                odd_solved(d).wait_send()

            @pl.when((q >= SLOW) & (q < LAST))
            def _():
                drain(d, 8)

            @pl.when((q >= SLOW) & (q < LAST))
            def _():
                drain(d, 7)

            @pl.when((q == LAST) | ((q >= 1) & (q < SLOW)))
            def _():
                drain(d, 6)

            @pl.when(q >= 1)
            def _():
                relay_even(d).wait_send()

            @pl.when(q > SLOW)
            def _():
                relay_odd(d).wait_send()


def shards(*arrays):
    anywhere = pl.BlockSpec(memory_space=pl.ANY)
    scalars = pl.BlockSpec(memory_space=pltpu.SMEM)
    dma, vmem = pltpu.SemaphoreType.DMA, pltpu.VMEM
    return pl.pallas_call(
        kernel,
        name="sweep",
        out_shape=jax.ShapeDtypeStruct((1, SOURCES, 1024), F32),
        in_specs=[anywhere] * 6 + [scalars] * 2,
        out_specs=pl.BlockSpec(memory_space=pltpu.VMEM),
        scratch_shapes=[
            vmem((SOURCES, 1024), F32),
            vmem((8, 128, 128), F32),
            vmem((SOURCES, 1024), F32),
            vmem((SOURCES, 1024), BF16),
            vmem((3, SOURCES, 1024), BF16),
            vmem((2, 8, 128, 1024), BF16),
            vmem((2, 8, 128, 1024), BF16),
            vmem((2, 8, 128, 1024), BF16),
            vmem((2, 8, 128, 1024), BF16),
            vmem((2, 8, 128, 1024), BF16),
            vmem((2, CHIPS, CHIPS, 256, 256), BF16),
            vmem((2, CHIPS, CHIPS, 256, 256), BF16),
            vmem((2, CHIPS, SOURCES, 256), F32),
            vmem((2, CHIPS, SOURCES, 256), F32),
            vmem((2, 8, SOURCES, 128), BF16),
            vmem((2, 2, 8, SOURCES, 128), BF16),
            vmem((2, 2, CHIPS, 2, SOURCES, 128), BF16),
            vmem((2, SOURCES, 1024), BF16),
            dma((6,)),
            dma((2,)),
            dma((2,)),
            dma((2,)),
            dma((2,)),
            dma((2, 2)),
            dma((2,)),
            dma((2,)),
            dma((2,)),
            dma((2, CHIPS)),
            dma(()),
            dma((2,)),
            dma((2, CHIPS)),
            dma((2, 2, CHIPS)),
            pltpu.SemaphoreType.REGULAR,
        ],
        compiler_params=pltpu.CompilerParams(
            collective_id=0, has_side_effects=True, vmem_limit_bytes=56 << 20
        ),
    )(*arrays)


def solution(mesh):
    in_specs = (
        P("layer", None, "plane"),
        P("layer", "plane", None, None),
        P("layer", None, None, "plane"),
        P("layer", None, None, "plane"),
        P("layer", None, None, "plane"),
        P("layer", None, None, "plane"),
        P("layer", None, "plane", None),
        P("layer", None, "plane", None),
    )
    return jax.shard_map(
        shards, mesh=mesh, in_specs=in_specs, out_specs=P("layer", None, "plane"), check_vma=False
    )
```

```python
import jax
import jax.numpy as jnp
from jax import lax
from jax.experimental import pallas as pl
from jax.experimental.pallas import tpu as pltpu
from jax.sharding import PartitionSpec as P

MESH = pl.DeviceIdType.MESH
BF16, F32 = jnp.bfloat16, jnp.float32
LAYERS, CHIPS, SOURCES = 32, 4, 16
LAST = LAYERS - 1
SEND_EARLY, MAKE_EARLY = 11, 14
SLOW = 3
NT = (((1,), (1,)), ((), ()))


def piece_row(ref):
    return jnp.concatenate([ref[j] for j in range(8)], axis=1)


def kernel(
    sources, fronts, down_left, down_right, up_left, up_right, ranks, pattern, out,
    src, tri, solved, solved_even, solved_odd, kept, even_right, odd_right, even_left, odd_left,
    even_step, odd_step, even_start, odd_start, even_in, pieces, sent,
    slow_sent, load_sem, kept_sem, left_sem, solved_sem, sent_sem, relay_sem, slow_sem,
    even_right_got, odd_right_got, even_left_got, solved_even_got, solved_odd_got, even_in_got, got, go_sem,
):
    layer, plane = lax.axis_index("layer"), lax.axis_index("plane")
    y, core = plane // 2, lax.rem(plane, 2)
    is_odd = core == 1
    odd_plane = 2 * y + 1
    upper = (layer >= LAYERS // 2).astype(jnp.int32)
    first, second = upper, 1 - upper
    lefts, rights = (down_left, up_left), (down_right, up_right)

    def sign(d):
        return 1 - 2 * d

    def position(d):
        return jnp.where(d == 0, layer, LAST - layer)

    def remote(source, target, send, got, to_layer, to_plane):
        return pltpu.make_async_remote_copy(
            source, target, send, got, device_id=(to_layer, to_plane), device_id_type=MESH
        )

    load_tri = pltpu.make_async_copy(fronts.at[0], tri, load_sem.at[0])
    load_src = pltpu.make_async_copy(sources.at[0], src, load_sem.at[1])
    def each(d, action):
        for way in range(2):
            pl.when(d == way)(lambda: action(way))

    def load_right(way):
        return pltpu.make_async_copy(rights[way].at[0], kept.at[way], load_sem.at[2 + way])

    def load_left(way):
        return pltpu.make_async_copy(lefts[way].at[0], odd_left.at[way], load_sem.at[4 + way])

    each(first, lambda way: load_right(way).start())
    load_tri.start()
    load_src.start()

    early = position(first)
    forward = sign(first)
    is_slow = (early >= 1) & (early <= SLOW)

    @pl.when(is_odd | is_slow)
    def _():
        each(first, lambda way: load_left(way).start())

    barrier = pltpu.get_barrier_semaphore()

    def greet(to_layer, to_plane):
        pl.semaphore_signal(barrier, inc=1, device_id=(to_layer, to_plane), device_id_type=MESH)

    def reach(r):
        return jnp.minimum(layer + r, LAST) - jnp.maximum(layer - r, 0) + 1

    @pl.when(is_odd)
    def _():
        for by in (-2, -1, 1, 2):

            @pl.when((layer + by >= 0) & (layer + by <= LAST))
            def _():
                for other in range(CHIPS):
                    greet(layer + by, 2 * other + 1)

        for turn in range(1, CHIPS):
            greet(layer, 2 * lax.rem(y + turn, CHIPS) + 1)
        for by in (-1, 0, 1):

            @pl.when((layer + by >= 0) & (layer + by <= LAST))
            def _():
                greet(layer + by, 2 * y)

        beside_slow = is_slow.astype(jnp.int32)
        past_slow = ((early >= 2) & (early <= SLOW + 1)).astype(jnp.int32)
        for turn in range(1, CHIPS):

            @pl.when(is_slow)
            def _():
                greet(layer, 2 * lax.rem(y + turn, CHIPS))

            @pl.when((early >= 2) & (early <= SLOW + 1))
            def _():
                greet(layer - forward, 2 * lax.rem(y + turn, CHIPS))

        pl.semaphore_wait(barrier, CHIPS * reach(2) - 1 + reach(1) + (CHIPS - 1) * (beside_slow + past_slow))

    @pl.when(core == 0)
    def _():
        for by in (-1, 0, 1):

            @pl.when((layer + by >= 0) & (layer + by <= LAST))
            def _():
                greet(layer + by, odd_plane)

        @pl.when(is_slow)
        def _():
            for turn in range(1, CHIPS):
                greet(layer, 2 * lax.rem(y + turn, CHIPS) + 1)
                greet(layer + forward, 2 * lax.rem(y + turn, CHIPS) + 1)

        @pl.when(early == 0)
        def _():
            greet(layer + forward, plane)

        @pl.when(early == 1)
        def _():
            greet(layer - forward, plane)

        pl.semaphore_wait(
            barrier, reach(1) + 2 * (CHIPS - 1) * is_slow.astype(jnp.int32) + (early <= 1).astype(jnp.int32)
        )

    def send_left(d):
        for way in range(2):

            @pl.when((core == 0) & (d == way) & (position(way) > SLOW))
            def _():
                for chip in range(CHIPS):
                    pair = pl.ds(2 * chip, 2)
                    remote(
                        lefts[way].at[0, pair], even_left.at[way, pair], left_sem.at[way], even_left_got.at[way, chip],
                        layer - sign(way), odd_plane,
                    ).start()

    def send_right(d):
        @pl.when(core == 0)
        def _():
            remote(kept.at[d], even_right.at[d], kept_sem.at[d], even_right_got.at[d], layer, odd_plane).start()

        @pl.when(is_odd & (position(d) >= SLOW) & (position(d) < LAST))
        def _():
            remote(
                kept.at[d], odd_right.at[d], kept_sem.at[d], odd_right_got.at[d], layer + sign(d), odd_plane
            ).start()

    def sent_factors(d):
        @pl.when((core == 0) & (position(d) > SLOW))
        def _():
            remote(even_left.at[d], even_left.at[d], left_sem.at[d], even_left_got.at[d, 0], layer, odd_plane).wait_send()

        @pl.when((core == 0) | ((position(d) >= SLOW) & (position(d) < LAST)))
        def _():
            remote(kept.at[d], even_right.at[d], kept_sem.at[d], even_right_got.at[d], layer, odd_plane).wait_send()

    def mask_right(d):
        for j in range(8):
            top = ranks[0, d, 0, j] * pattern[0, d, 0, j]
            rows = lax.broadcasted_iota(jnp.int32, (128, 1024), 0)
            kept[d, j] = jnp.where(rows < top, kept[d, j].astype(F32), 0.0).astype(BF16)

    send_left(first)
    each(first, lambda way: load_right(way).wait())
    mask_right(first)
    send_right(first)
    each(second, lambda way: load_right(way).start())

    @pl.when(is_odd)
    def _():
        each(second, lambda way: load_left(way).start())

    load_tri.wait()
    load_src.wait()
    row = lax.broadcasted_iota(jnp.int32, (128, 128), 0)
    col = lax.broadcasted_iota(jnp.int32, (128, 128), 1)

    def exact(a, b):
        return jnp.dot(a, b, preferred_element_type=F32, precision=lax.Precision.HIGHEST)

    by_col, units, inverses = [], [], []
    for b in range(8):
        block = tri[b]
        diagonal = jnp.where(row == col, block, 0.0)
        by_row = 1.0 / jnp.sum(diagonal, axis=1, keepdims=True)
        by_col.append(1.0 / jnp.sum(diagonal, axis=0, keepdims=True))
        units.append(jnp.where(row > col, block * by_row, 0.0))
        inverses.append(jnp.where(row == col, 1.0, 0.0))
    for half in (1, 2, 4, 8, 16, 32, 64):
        joins = (row // (2 * half) == col // (2 * half)) & (row // half != col // half)
        for b in range(8):
            part = jnp.where(joins, units[b], 0.0)
            if half > 1:
                part = exact(inverses[b], exact(part, inverses[b]))
            inverses[b] = inverses[b] - part
    for b in range(8):
        solved[:, 128 * b : 128 * (b + 1)] = lax.dot_general(
            src[:, 128 * b : 128 * (b + 1)] * by_col[b], inverses[b], NT,
            preferred_element_type=F32, precision=lax.Precision.HIGHEST,
        )
    sent_solved = solved_odd.at[2]
    sent_solved[...] = solved[...].astype(BF16)
    even_solved = remote(sent_solved, solved_even, solved_sem.at[0], solved_even_got, layer, odd_plane)

    def odd_solved(d):
        return remote(
            sent_solved, solved_odd.at[d], solved_sem.at[d], solved_odd_got.at[d], layer + sign(d), odd_plane
        )

    def sends_solved(d):
        return is_odd & (position(d) < LAST) & ((position(d) == 0) | (position(d) >= SLOW))

    def slow_even(source):
        return remote(source, solved_even, slow_sem.at[0], solved_even_got, layer + forward, 2 * y)

    def slow_odd(source):
        return remote(
            source, solved_odd.at[first], slow_sem.at[1], solved_odd_got.at[first], layer + forward, odd_plane
        )

    @pl.when((core == 0) & (early == 0))
    def _():
        slow_even(sent_solved).start()

    @pl.when(core == 0)
    def _():
        even_solved.start()

    for d in range(2):

        @pl.when(sends_solved(d))
        def _():
            odd_solved(d).start()

    each(second, lambda way: load_right(way).wait())
    mask_right(second)

    def send_second():
        sent_factors(first)
        send_left(second)
        send_right(second)

    def open_way(d):
        each(d, lambda way: load_left(way).wait())

        @pl.when(position(d) >= 1)
        def _():
            remote(sent_solved, solved_odd.at[d], solved_sem.at[d], solved_odd_got.at[d], layer, odd_plane).wait_recv()
            begin = lax.dot_general(
                solved_odd[d], odd_left[d].reshape(1024, 1024), NT, preferred_element_type=F32
            )
            for chip in range(CHIPS):
                odd_start[d, chip] = begin[:, 256 * chip : 256 * (chip + 1)]

    def wait_even_right(d):
        remote(kept.at[d], even_right.at[d], kept_sem.at[d], even_right_got.at[d], layer, odd_plane).wait_recv()

    def make(right, left, d, chip, step):
        block = left[d, pl.ds(2 * chip, 2)].reshape(256, 1024)
        full = right[d].reshape(1024, 1024)
        columns = lax.dot_general(full, block, NT, preferred_element_type=F32).astype(BF16)
        step[d, chip] = columns.reshape(CHIPS, 256, 256)

    def wait_odd_right(d):
        remote(kept.at[d], odd_right.at[d], kept_sem.at[d], odd_right_got.at[d], layer, odd_plane).wait_recv()

    def make_odd(d):
        @pl.when(position(d) > SLOW)
        def _():
            wait_odd_right(d)

            @pl.loop(0, CHIPS)
            def _(chip):
                make(odd_right, odd_left, d, chip, odd_step)

    def wait_even_left(d, chip):
        part = even_left.at[d, pl.ds(2 * chip, 2)]
        remote(part, part, left_sem.at[d], even_left_got.at[d, chip], layer, odd_plane).wait_recv()

    def make_even(d):
        @pl.when((position(d) > SLOW + 1) & (position(d) < LAST))
        def _():
            @pl.loop(0, CHIPS)
            def _(chip):
                wait_even_left(d, chip)
                block = even_left[d, pl.ds(2 * chip, 2)].reshape(256, 1024)
                even_start[d, chip] = lax.dot_general(solved_even[...], block, NT, preferred_element_type=F32)
                make(even_right, even_left, d, chip, even_step)

    def wait_pieces(ref, got, count):
        remote(ref.at[pl.ds(0, count)], ref.at[pl.ds(0, count)], sent_sem.at[0], got, layer, odd_plane).wait_recv()

    def pair_row(ref, chip):
        return jnp.concatenate([ref[2 * chip], ref[2 * chip + 1]], axis=1)

    def start_only(d, start, deliver):
        for turn in (2, 1, 3, 0):
            other = lax.rem(y + turn, CHIPS)
            deliver(turn, other, start[d, other].astype(BF16))

    last_y, first_y = (y == CHIPS - 1).astype(jnp.int32), (y == 0).astype(jnp.int32)
    comes = (0, 1 + 2 * last_y, 3 - last_y, 2 - last_y)
    goes = (2 + first_y, 1 + first_y, 3 - 2 * first_y, 0)

    def chip_at(turn):
        return lax.rem(y + turn, CHIPS)

    def seen(turn):
        return lax.rem(CHIPS - turn, CHIPS)

    def wait_from(ref, got, turn, count):
        wait_pieces(ref, got.at[turn], count)

    def wait_all(ref, got, own):
        for turn in range(CHIPS):
            wait_from(ref, got, turn, own if turn == 0 else 2)

    def advance(d, ref, got, own, step, start, deliver):
        totals = [start[d, chip_at(turn)] for turn in goes]
        for at, source in enumerate(comes):
            if at != 1:
                wait_from(ref, got, source, own if at == 0 else 2)
            if at == 0:
                wait_from(ref, got, comes[1], 2)
            values = pair_row(ref, chip_at(source))
            for index, turn in enumerate(goes):
                totals[index] += jnp.dot(
                    values, step[d, chip_at(turn), chip_at(source)], preferred_element_type=F32
                )
                if at == CHIPS - 1:
                    deliver(turn, chip_at(turn), totals[index].astype(BF16))

    def odd_deliver(d):
        q = position(d)
        direct = (q == LAST) | (q < SLOW)
        kind = direct.astype(jnp.int32)
        odd_layer = layer + (1 - kind) * sign(d)

        def deliver(turn, other, result):
            for part in range(2):
                sent[d, 1, other, part] = result[:, 128 * part : 128 * (part + 1)]
            if isinstance(turn, int) and turn == 0:
                even_in[d, odd_plane] = result[:, :128]
            else:
                remote(
                    sent.at[d, 1, other, 0], even_in.at[d, odd_plane], sent_sem.at[d], even_in_got.at[d, seen(turn)],
                    layer, 2 * other + 1,
                ).start()

            odd_part = remote(
                sent.at[d, 1, other, 1], pieces.at[kind, d, odd_plane], sent_sem.at[d], got.at[kind, d, seen(turn)],
                odd_layer, 2 * other + 1,
            )
            if not isinstance(turn, int) or turn != 0:
                odd_part.start()
            else:
                pl.when(jnp.logical_not(direct))(odd_part.start)

                @pl.when(direct)
                def _():
                    pieces[1, d, odd_plane] = result[:, 128:]

        return deliver

    def run_odd(d):
        @pl.when(position(d) > SLOW)
        def _():
            advance(d, pieces.at[0, d], got.at[0, d], 2, odd_step, odd_start, odd_deliver(d))

    def even_deliver(d):
        kind = (position(d) == LAST - 1).astype(jnp.int32)

        def deliver(turn, other, result):
            for part in range(2):
                sent[d, 0, other, part] = result[:, 128 * part : 128 * (part + 1)]
            remote(
                sent.at[d, 0, other, 0], even_in.at[d, 2 * y], sent_sem.at[d], even_in_got.at[d, seen(turn)],
                layer + sign(d), 2 * other + 1,
            ).start()

            remote(
                sent.at[d, 0, other, 1], pieces.at[kind, d, 2 * y], sent_sem.at[d], got.at[kind, d, seen(turn)],
                layer + (2 - kind) * sign(d), 2 * other + 1,
            ).start()

        return deliver

    def run_even(d):
        q = position(d)

        @pl.when((q > SLOW + 1) & (q < LAST))
        def _():
            advance(
                d, even_in.at[d], even_in_got.at[d], 1, even_step, even_start,
                even_deliver(d),
            )

        @pl.when(q == LAST)
        def _():
            wait_all(even_in.at[d], even_in_got.at[d], 1)

    def slow_deliver(turn, other, result):
        for part in range(2):
            sent[first, 0, other, part] = result[:, 128 * part : 128 * (part + 1)]
        remote(
            sent.at[first, 0, other, 0], even_in.at[first, 2 * y], sent_sem.at[first],
            even_in_got.at[first, seen(turn)], layer, 2 * other + 1,
        ).start()

        kind = (early < SLOW).astype(jnp.int32)
        remote(
            sent.at[first, 0, other, 1], pieces.at[kind, first, 2 * y], sent_sem.at[first],
            got.at[kind, first, seen(turn)], layer + (1 - kind) * forward, 2 * other + 1,
        ).start()

    @pl.when((core == 0) & is_slow)
    def _():
        each(first, lambda way: load_left(way).wait())
        remote(sent_solved, solved_even, solved_sem.at[0], solved_even_got, layer, 2 * y).wait_recv()
        for turn in (2, 1, 3, 0):
            other = lax.rem(y + turn, CHIPS)
            block = odd_left[first, pl.ds(2 * other, 2)].reshape(256, 1024)
            result = lax.dot_general(solved_even[...], block, NT, preferred_element_type=F32)
            slow_deliver(turn, other, result.astype(BF16))

    def join(ref, right, left, part, deliver):
        trace = jnp.dot(piece_row(ref), right[first].reshape(1024, 1024), preferred_element_type=F32)
        whole = (part.astype(F32) + trace).astype(BF16)
        for turn in (2, 1, 3, 0):
            other = lax.rem(y + turn, CHIPS)
            block = left[first, pl.ds(2 * other, 2)].reshape(256, 1024)
            deliver(turn, other, lax.dot_general(whole, block, NT, preferred_element_type=F32).astype(BF16))

    def join_odd():
        wait_odd_right(first)
        wait_all(pieces.at[0, first], got.at[0, first], 2)
        join(pieces.at[0, first], odd_right, odd_left, solved_odd[first], odd_deliver(first))

    def join_even():
        for chip in range(CHIPS):
            wait_even_left(first, chip)
        wait_all(even_in.at[first], even_in_got.at[first], 1)
        join(even_in.at[first], even_right, even_left, solved_even[...], even_deliver(first))

    def slow_step():
        wait_all(even_in.at[first], even_in_got.at[first], 1)
        trace = jnp.dot(
            piece_row(even_in.at[first]), even_right[first].reshape(1024, 1024), preferred_element_type=F32
        )
        slow_sent[0] = (solved_even[...].astype(F32) + trace).astype(BF16)
        slow_even(slow_sent.at[0]).start()
        wait_all(pieces.at[1, first], got.at[1, first], 1)
        trace = jnp.dot(
            piece_row(pieces.at[1, first]), kept[first].reshape(1024, 1024), preferred_element_type=F32
        )
        slow_sent[1] = (solved[...] + trace).astype(BF16)
        slow_odd(slow_sent.at[1]).start()

    def relay_even(d):
        return remote(even_in.at[d], pieces.at[1, d], relay_sem.at[0, d], got.at[1, d, 0], layer, 2 * y)

    def relay_odd(d):
        return remote(pieces.at[0, d], pieces.at[1, d], relay_sem.at[1, d], got.at[1, d, 0], layer - sign(d), odd_plane)

    def sweep(d):
        q = position(d)
        run_even(d)

        @pl.when(q >= 1)
        def _():
            relay_even(d).start()

        @pl.when(q > SLOW)
        def _():
            relay_odd(d).start()

    @pl.when(is_odd)
    def _():
        remote(sent_solved, solved_even, solved_sem.at[0], solved_even_got, layer, odd_plane).wait_recv()
        wait_even_right(first)
        open_way(first)

        @pl.when(is_slow)
        def _():
            start_only(first, odd_start, odd_deliver(first))

        @pl.when((early >= 1) & (early < SLOW))
        def _():
            slow_step()

        @pl.when(position(first) >= SEND_EARLY)
        def _():
            send_second()

        @pl.when(early == SLOW + 1)
        def _():
            join_odd()

        @pl.when((early == SLOW) | (early == SLOW + 1))
        def _():
            join_even()

        @pl.when(early > SLOW + 1)
        def _():
            make_odd(first)

        @pl.when(early == SLOW + 2)
        def _():
            run_odd(first)

        make_even(first)

        @pl.when(position(first) >= MAKE_EARLY)
        def _():
            wait_even_right(second)
            open_way(second)
            make_odd(second)
            make_even(second)

        @pl.when(early > SLOW + 2)
        def _():
            run_odd(first)

        sweep(first)

        @pl.when(position(first) < SEND_EARLY)
        def _():
            pl.semaphore_signal(go_sem, inc=1, device_id=(layer, 2 * y), device_id_type=MESH)
            send_second()

        @pl.when(position(first) < MAKE_EARLY)
        def _():
            wait_even_right(second)
            open_way(second)
            make_odd(second)
            make_even(second)

        run_odd(second)
        sweep(second)

    @pl.when(core == 0)
    def _():
        @pl.when(position(first) < SEND_EARLY)
        def _():
            pl.semaphore_wait(go_sem, 1)

        send_second()

    def add_own(d):
        q = position(d)

        @pl.when(q >= 1)
        def _():
            @pl.when(is_odd & (q == LAST))
            def _():
                wait_all(pieces.at[1, d], got.at[1, d], 1)

            @pl.when((core == 0) | ((q >= SLOW) & (q < LAST)))
            def _():
                wait_pieces(pieces.at[1, d], got.at[1, d, 0], 8)

            solved[...] += jnp.dot(
                piece_row(pieces.at[1, d]), kept[d].reshape(1024, 1024), preferred_element_type=F32
            )

    add_own(first)
    add_own(second)
    out[0] = solved[...]

    sent_factors(second)

    def drain(d, count):
        part = pieces.at[0, d, pl.ds(0, count)]
        remote(part, part, sent_sem.at[d], got.at[1, d, 0], layer, odd_plane).wait_send()

    @pl.when(core == 0)
    def _():
        even_solved.wait_send()

        @pl.when(early == 0)
        def _():
            slow_even(sent_solved).wait_send()

        @pl.when(is_slow)
        def _():
            drain(first, 8)

    @pl.when(is_odd)
    def _():
        @pl.when((early >= 1) & (early < SLOW))
        def _():
            slow_even(slow_sent.at[0]).wait_send()
            slow_odd(slow_sent.at[1]).wait_send()

        for d in range(2):
            q = position(d)

            @pl.when(sends_solved(d))
            def _():
                odd_solved(d).wait_send()

            @pl.when((q >= SLOW) & (q < LAST))
            def _():
                drain(d, 8)

            @pl.when((q >= SLOW) & (q < LAST))
            def _():
                drain(d, 7)

            @pl.when((q == LAST) | ((q >= 1) & (q < SLOW)))
            def _():
                drain(d, 6)

            @pl.when(q >= 1)
            def _():
                relay_even(d).wait_send()

            @pl.when(q > SLOW)
            def _():
                relay_odd(d).wait_send()


def shards(*arrays):
    anywhere = pl.BlockSpec(memory_space=pl.ANY)
    scalars = pl.BlockSpec(memory_space=pltpu.SMEM)
    dma, vmem = pltpu.SemaphoreType.DMA, pltpu.VMEM
    return pl.pallas_call(
        kernel,
        name="sweep",
        out_shape=jax.ShapeDtypeStruct((1, SOURCES, 1024), F32),
        in_specs=[anywhere] * 6 + [scalars] * 2,
        out_specs=pl.BlockSpec(memory_space=pltpu.VMEM),
        scratch_shapes=[
            vmem((SOURCES, 1024), F32),
            vmem((8, 128, 128), F32),
            vmem((SOURCES, 1024), F32),
            vmem((SOURCES, 1024), BF16),
            vmem((3, SOURCES, 1024), BF16),
            vmem((2, 8, 128, 1024), BF16),
            vmem((2, 8, 128, 1024), BF16),
            vmem((2, 8, 128, 1024), BF16),
            vmem((2, 8, 128, 1024), BF16),
            vmem((2, 8, 128, 1024), BF16),
            vmem((2, CHIPS, CHIPS, 256, 256), BF16),
            vmem((2, CHIPS, CHIPS, 256, 256), BF16),
            vmem((2, CHIPS, SOURCES, 256), F32),
            vmem((2, CHIPS, SOURCES, 256), F32),
            vmem((2, 8, SOURCES, 128), BF16),
            vmem((2, 2, 8, SOURCES, 128), BF16),
            vmem((2, 2, CHIPS, 2, SOURCES, 128), BF16),
            vmem((2, SOURCES, 1024), BF16),
            dma((6,)),
            dma((2,)),
            dma((2,)),
            dma((2,)),
            dma((2,)),
            dma((2, 2)),
            dma((2,)),
            dma((2,)),
            dma((2,)),
            dma((2, CHIPS)),
            dma(()),
            dma((2,)),
            dma((2, CHIPS)),
            dma((2, 2, CHIPS)),
            pltpu.SemaphoreType.REGULAR,
        ],
        compiler_params=pltpu.CompilerParams(
            collective_id=0, has_side_effects=True, vmem_limit_bytes=56 << 20
        ),
    )(*arrays)


def solution(mesh):
    in_specs = (
        P("layer", None, "plane"),
        P("layer", "plane", None, None),
        P("layer", None, None, "plane"),
        P("layer", None, None, "plane"),
        P("layer", None, None, "plane"),
        P("layer", None, None, "plane"),
        P("layer", None, "plane", None),
        P("layer", None, "plane", None),
    )
    return jax.shard_map(
        shards, mesh=mesh, in_specs=in_specs, out_specs=P("layer", None, "plane"), check_vma=False
    )
```
